256 devices in a mesh: aa: 8 (over x, core), ba: 32 (over z, y).
Axes of the slice: x: 4, y: 4, z: 8, core: 2. Of those that a mesh axis runs over, the one named last changes fastest.
Arguments:
- tokens: bfloat16 [262144, 2048], P(('aa', 'ba')), may hold values from -42 to 42
- grad_out: bfloat16 [262144, 1024], P(('aa', 'ba')), may hold values from -6 to 6
- master_weight: float32 [2048, 1024], P(('aa', 'ba')), may hold values from -0.003 to 0.003
- first_moment: float32 [2048, 1024], P(('aa', 'ba')), may hold values from -0.6 to 0.6
- second_moment: float32 [2048, 1024], P(('aa', 'ba')), may hold values from 0.02 to 0.2
- next_tokens: bfloat16 [262144, 2048], P(('aa', 'ba')), may hold values from -72 to 72
Outputs:
- new_first: float32 [2048, 1024], P(('aa', 'ba'))
- new_second: float32 [2048, 1024], P(('aa', 'ba'))
- next_hidden: bfloat16 [262144, 512], P(('aa', 'ba'))
The draws below stay inside these ranges and needn't reach their ends.
All inputs are finite; a program needn't handle non-finite values.
Results may differ from the reference program's by a relative error of at most 0.0064.
Values may be sent and summed in bfloat16 or wider, within the bound.
A program may use at most 64 MiB of HBM per device.

```python
import math
import jax
import jax.numpy as jnp
from jax import lax

D = 2048
FF = 512
QB = 128
TOK_DEV = 1024
TOKENS = 262144
N_AA = 8
N_BA = 32


def coherent_rows(key):
    sign_key, level_key = jax.random.split(jax.random.fold_in(key, 1031))
    row_sign = jnp.where(jax.random.bernoulli(sign_key, 0.5, (TOKENS, 1)), 1.0, -1.0).astype(jnp.float32)
    row_level = jnp.exp(jax.random.uniform(level_key, (N_AA * N_BA, 1), jnp.float32, -math.log(3.0), math.log(3.0)))
    row_level = jnp.repeat(row_level, TOK_DEV, axis=0)
    strength = (1.7 / TOKENS) ** 0.25
    return row_sign * row_level * strength


def draw_tokens(key, part):
    first_key = jax.random.fold_in(jax.random.fold_in(key, 7), 0)
    second_key = jax.random.fold_in(jax.random.fold_in(key, 7), 1)
    pick_key = jax.random.fold_in(jax.random.fold_in(key, 7), 3)
    size_key = jax.random.fold_in(jax.random.fold_in(key, 7), 4)
    turn_key = jax.random.fold_in(jax.random.fold_in(key, 7), 5)
    column = jnp.arange(D, dtype=jnp.float32)
    rising = 1.0 + 2.0 * column / D
    chosen = jax.random.permutation(pick_key, D) < D // 8
    magnitude = jax.random.uniform(size_key, (D,), jnp.float32, 0.5, 1.5)
    magnitude = magnitude * jnp.where(jax.random.bernoulli(turn_key, 0.5, (D,)), 1.0, -1.0)
    spread = jnp.exp(jax.random.uniform(second_key, (D,), jnp.float32, 0.0, jnp.log(3.5)))
    sample = jnp.clip(jax.random.normal(first_key, (TOKENS, D), jnp.float32), -4.0, 4.0)
    direction = jnp.where(chosen, magnitude * rising * spread, 0.0)
    values = sample * rising * spread + coherent_rows(key) * direction[None, :]
    return jnp.clip(values, -42.0, 42.0).astype(jnp.bfloat16)


def draw_grad_out(key, part):
    noise_key, size_key, turn_key = jax.random.split(jax.random.fold_in(key, 13), 3)
    magnitude = jax.random.uniform(size_key, (2 * FF,), jnp.float32, 0.5, 1.5)
    magnitude = magnitude * jnp.where(jax.random.bernoulli(turn_key, 0.5, (2 * FF,)), 1.0, -1.0)
    coherent = coherent_rows(key) * magnitude[None, :]
    sample = jnp.clip(jax.random.normal(noise_key, (TOKENS, 2 * FF), jnp.float32), -6.0, 6.0)
    values = sample + coherent
    return jnp.clip(values, -6.0, 6.0).astype(jnp.bfloat16)


def block_levels(own_key, extent, cuts, least, high):
    gain = 1.0
    for axis_at, blocks in cuts:
        heights = jax.random.uniform(jax.random.fold_in(jax.random.fold_in(own_key, 6), axis_at), (blocks,), jnp.float32, least / len(cuts), high / len(cuts))
        gain = gain * jnp.repeat(jnp.exp(heights), extent[axis_at] // blocks).reshape((-1,) + (1,) * (len(extent) - 1 - axis_at))
    return gain


def noise(stream_key, dims, scale, bound, shards=(), kind=jnp.bfloat16):
    factor_of = block_levels(stream_key, dims, shards, -0.22, 0.18) if shards else 1.0
    entries = jax.random.normal(stream_key, dims, jnp.float32) * scale * factor_of
    return jnp.minimum(jnp.maximum(entries, -bound), bound).astype(kind)


def setup_inputs(seed: int = 0) -> dict:
    streams_of = jax.random.split(jax.random.key(seed), 7)
    tokens = draw_tokens(jax.random.fold_in(streams_of[6], 71), 0)
    grad_out = draw_grad_out(jax.random.fold_in(streams_of[6], 71), 0)
    master_weight = noise(streams_of[2], (D, 2 * FF), 0.0005, 0.003, ((0, 256),), jnp.float32)
    first_moment = noise(streams_of[3], (D, 2 * FF), 0.1, 0.6, ((0, 256),), jnp.float32)
    second_moment = jnp.clip(jnp.exp(math.log(0.2) - 2.3025851 * jax.random.uniform(streams_of[4], (D, 2 * FF), jnp.float32) ** block_levels(streams_of[4], (D, 2 * FF), ((0, 256),), -0.2, 0.2)), 0.02, 0.2)
    next_tokens = noise(streams_of[5], (TOKENS, D), 12.0, 72.0, ((0, 256),))
    return {"tokens": tokens, "grad_out": grad_out, "master_weight": master_weight, "first_moment": first_moment, "second_moment": second_moment, "next_tokens": next_tokens}


def encode(matrix):
    height, width = matrix.shape
    blocks = matrix.reshape(height, width // QB, QB)
    largest = lax.optimization_barrier(jnp.max(jnp.abs(blocks), axis=2))
    scales = ((largest + 1e-06) / 448.0).astype(jnp.bfloat16)
    codes = (blocks / scales.astype(jnp.float32)[:, :, None]).astype(jnp.bfloat16)
    return (codes, scales)

def decode(codes, scales):
    height = codes.shape[0]
    values = codes.astype(jnp.float32) * scales.astype(jnp.float32)[:, :, None]
    return values.reshape(height, codes.shape[1] * codes.shape[2])

def reference(tokens, grad_out, master_weight, first_moment, second_moment, next_tokens):
    inputs = tokens.reshape(N_AA, N_BA, TOK_DEV, D)
    cotangents = grad_out.reshape(N_AA, N_BA, TOK_DEV, 2 * FF)

    def outer_step(total, inner_index):

        def inner_step(partial_value, outer_index):
            chosen = inputs[outer_index, inner_index]
            chosen_cot = cotangents[outer_index, inner_index]
            local_grad = jnp.dot(chosen.T, chosen_cot, preferred_element_type=jnp.float32)
            codes, scales = encode(local_grad)
            return (partial_value + decode(codes, scales), None)
        partial_value, unused = lax.scan(inner_step, jnp.zeros((D, 2 * FF), jnp.float32), jnp.arange(N_AA, dtype=jnp.int32))
        codes, scales = encode(partial_value)
        return (total + decode(codes, scales), None)
    gradient, unused = lax.scan(outer_step, jnp.zeros((D, 2 * FF), jnp.float32), jnp.arange(N_BA, dtype=jnp.int32))
    gate_sq = jnp.sum(gradient[:, :FF] * gradient[:, :FF])
    up_sq = jnp.sum(gradient[:, FF:] * gradient[:, FF:])
    limit = math.sqrt(D * FF)
    gate_factor = jnp.minimum(1.0, limit / jnp.sqrt(gate_sq + 1e-06))
    up_factor = jnp.minimum(1.0, limit / jnp.sqrt(up_sq + 1e-06))
    clipped = jnp.concatenate([gradient[:, :FF] * gate_factor, gradient[:, FF:] * up_factor], axis=1)
    new_first = 0.9 * first_moment + 0.1 * clipped
    new_second = 0.95 * second_moment + 0.05 * clipped * clipped
    corr_first = 1.0 - 0.9 ** 10
    corr_second = 1.0 - 0.95 ** 10
    updated = master_weight * (1.0 - 0.003 * 0.1) - 0.003 * (new_first / corr_first) / (jnp.sqrt(new_second / corr_second) + 1e-08)
    low_weight = updated.astype(jnp.bfloat16)
    projected = jnp.dot(next_tokens, low_weight, preferred_element_type=jnp.float32)
    next_hidden = (jax.nn.silu(projected[:, :FF]) * projected[:, FF:]).astype(jnp.bfloat16)
    return (new_first, new_second, next_hidden)
```

```python
import functools
import math

import jax
import jax.numpy as jnp
from jax import lax
from jax.experimental import pallas as pl
from jax.experimental.pallas import tpu as pltpu
from jax.sharding import Mesh
from jax.sharding import PartitionSpec as P

NX, NC, NZ, NY = 4, 2, 8, 4
ROWS = 8
D = 2048
FF = 512
TOK = 1024
AXES = ("x", "c", "z", "y")
MESH = pl.DeviceIdType.MESH
f32 = jnp.float32
bf16 = jnp.bfloat16


def body(
    tok_hbm, cot_hbm, w_ref, m_ref, v_ref, nxt_hbm,
    nf_ref, nv_ref, out_ref,
    tok, cot, nxt, own, give, take,
    sa, sb, ra1, rb1, ta, tb, ra2, rb2, tz, rz, sq, rsq_z, rsq_y, rsq_x, rsq_c,
    wz, rwz, wa, wb,
    ld, core_s, core_r, a1_s, a1_r, b1_s, b1_r, a2_s, a2_r, b2_s, b2_r, z_s, z_r,
    qz_s, qz_r, qy_s, qy_r, qx_s, qx_r, qc_s, qc_r,
    gz_s, gz_r, ga2_s, ga2_r, gb2_s, gb2_r, ga3_s, ga3_r, gb3_s, gb3_r, gca_s, gca_r, gcb_s, gcb_r,
):
    x, c, z, y = (lax.axis_index(a) for a in AXES)
    other = 1 - c

    def xp(o):
        return {"x": lax.rem(x + o, NX)}

    def yp(o):
        return {"y": lax.rem(y + o, NY)}

    def zp(o):
        return {"z": lax.rem(z + o, NZ)}

    mate = {"c": other}
    peers = [mate] + [xp(o) for o in range(1, NX)] + [yp(o) for o in range(1, NY)] + [zp(o) for o in range(1, NZ)]

    def send(src, dst, ss, rs, to):
        cp = pltpu.make_async_remote_copy(
            src_ref=src, dst_ref=dst, send_sem=ss, recv_sem=rs, device_id=to, device_id_type=MESH
        )
        cp.start()
        return cp

    barrier = pltpu.get_barrier_semaphore()
    for p in peers:
        pl.semaphore_signal(barrier, inc=1, device_id=p, device_id_type=MESH)

    loads = [
        pltpu.make_async_copy(cot_hbm, cot, ld.at[0]),
        pltpu.make_async_copy(tok_hbm, tok, ld.at[1]),
        pltpu.make_async_copy(nxt_hbm, nxt, ld.at[2]),
    ]
    for cp in loads:
        cp.start()
    loads[0].wait()
    loads[1].wait()

    offs = (2, 1, 3, 0)
    blocks = [lax.rem(x + o, NX) for o in offs]

    def block_grad(xb, cc):
        start = pl.multiple_of(xb * 512 + cc * 256, 256)
        return lax.dot_general(
            tok[:, pl.ds(start, 256)], cot[...], (((0,), (0,)), ((), ())), preferred_element_type=f32
        )

    pending = []
    core = []
    for j in range(NX):
        xb = blocks[j]
        give[j] = block_grad(xb, other).astype(bf16).reshape(NZ, NY, ROWS, 2 * FF)
        if j == 0:
            pl.semaphore_wait(barrier, len(peers))
        core.append(send(give.at[j], take.at[j], core_s.at[j], core_r.at[j], mate))
        own[j] = block_grad(xb, c).reshape(NZ, NY, ROWS, 2 * FF)

    a1, b1 = [], []
    for j in range(NX):
        xb, o = blocks[j], offs[j]
        core[j].wait()
        total = own[j] + take[j].astype(f32)
        sa[j] = total[:, :, :, :FF].astype(bf16)
        half = total[:, :, :, FF:].astype(bf16)
        for k in range(NY):
            sb[k, xb] = half[:, k]
        if o:
            a1.append(send(sa.at[j], ra1.at[o - 1], a1_s.at[o - 1], a1_r.at[o - 1], xp(o)))
        for k in range(1, NY):
            yk = lax.rem(y + k, NY)
            b1.append(send(sb.at[yk, xb], rb1.at[k - 1, xb], b1_s.at[k - 1, j], b1_r.at[k - 1, j], yp(k)))
    for cp in a1 + b1:
        cp.wait()

    total = sa[NX - 1].astype(f32)
    for k in range(NX - 1):
        total += ra1[k].astype(f32)
    total = total.astype(bf16)
    for k in range(NY):
        ta[k] = total[:, k]
    for i in range(NX):
        total = sb[y, i].astype(f32)
        for k in range(NY - 1):
            total += rb1[k, i].astype(f32)
        tb[i] = total.astype(bf16)

    st2 = []
    for o in range(1, NY):
        st2.append(send(ta.at[lax.rem(y + o, NY)], ra2.at[o - 1], a2_s.at[o - 1], a2_r.at[o - 1], yp(o)))
        st2.append(send(tb.at[lax.rem(x + o, NX)], rb2.at[o - 1], b2_s.at[o - 1], b2_r.at[o - 1], xp(o)))
    for cp in st2:
        cp.wait()
    total = ta[y].astype(f32)
    for k in range(NY - 1):
        total += ra2[k].astype(f32)
    tz[:, :, :FF] = total.astype(bf16)
    total = tb[x].astype(f32)
    for k in range(NX - 1):
        total += rb2[k].astype(f32)
    tz[:, :, FF:] = total.astype(bf16)

    st3 = []
    for o in range(1, NZ):
        st3.append(send(tz.at[lax.rem(z + o, NZ)], rz.at[o - 1], z_s.at[o - 1], z_r.at[o - 1], zp(o)))
    for cp in st3:
        cp.wait()
    grad = tz[z].astype(f32)
    for k in range(NZ - 1):
        grad += rz[k].astype(f32)

    def fold(t):
        t = t * t
        t = jnp.sum(t, axis=0, keepdims=True)
        return t[:, 0:128] + t[:, 128:256] + t[:, 256:384] + t[:, 384:512]

    def everyone(stage, slots, ss, rs, peer, n):
        cps = [send(sq.at[stage], slots.at[o - 1], ss.at[o - 1], rs.at[o - 1], peer(o)) for o in range(1, n)]
        for cp in cps:
            cp.wait()
        t = sq[stage]
        for k in range(n - 1):
            t = t + slots[k]
        return t

    sq[0] = jnp.concatenate([fold(grad[:, :FF]), fold(grad[:, FF:])], axis=0)
    sq[1] = everyone(0, rsq_z, qz_s, qz_r, zp, NZ)
    sq[2] = everyone(1, rsq_y, qy_s, qy_r, yp, NY)
    sq[3] = everyone(2, rsq_x, qx_s, qx_r, xp, NX)
    both = everyone(3, rsq_c, qc_s, qc_r, lambda o: mate, NC)
    limit = math.sqrt(D * FF)
    factor = jnp.minimum(1.0, limit / jnp.sqrt(jnp.sum(both, axis=1, keepdims=True) + 1e-06))
    gate_factor, up_factor = factor[0:1], factor[1:2]
    clipped = jnp.concatenate([grad[:, :FF] * gate_factor, grad[:, FF:] * up_factor], axis=1)
    new_first = 0.9 * m_ref[...] + 0.1 * clipped
    new_second = 0.95 * v_ref[...] + 0.05 * clipped * clipped
    nf_ref[...] = new_first
    nv_ref[...] = new_second
    corr_first = 1.0 - 0.9**10
    corr_second = 1.0 - 0.95**10
    updated = w_ref[...] * (1.0 - 0.003 * 0.1) - 0.003 * (new_first / corr_first) / (
        jnp.sqrt(new_second / corr_second) + 1e-08
    )
    wz[...] = updated.astype(bf16)

    cps = [send(wz, rwz.at[z], gz_s.at[o - 1], gz_r.at[o - 1], zp(o)) for o in range(1, NZ)]
    rwz[z] = wz[...]
    for cp in cps:
        cp.wait()
    wa[x, c, :, y] = rwz[:, :, :FF]
    wb[x, c, :, y] = rwz[:, :, FF:]
    g2 = []
    for o in range(1, NY):
        g2.append(send(wa.at[x, c, :, y], wa.at[x, c, :, y], ga2_s.at[o - 1], ga2_r.at[o - 1], yp(o)))
        g2.append(send(wb.at[x, c, :, y], wb.at[x, c, :, y], gb2_s.at[o - 1], gb2_r.at[o - 1], xp(o)))
    for cp in g2:
        cp.wait()
    g3 = []
    last = []
    for o in (2, 1, 3):
        g3.append((o, send(wa.at[x, c], wa.at[x, c], ga3_s.at[o - 1], ga3_r.at[o - 1], xp(o)),
                   send(wb.at[:, c, :, y], wb.at[:, c, :, y], gb3_s.at[o - 1], gb3_r.at[o - 1], yp(o))))
    last.append(send(wa.at[x, c], wa.at[x, c], gca_s.at[0], gca_r.at[0], mate))
    last.append(send(wb.at[:, c, :, y], wb.at[:, c, :, y], gcb_s.at[0], gcb_r.at[0], mate))
    for o, ca, cb in (g3[1], g3[2], g3[0]):
        ca.wait()
        xs = lax.rem(x - o + NX, NX)
        last.append(send(wa.at[xs, c], wa.at[xs, c], gca_s.at[o], gca_r.at[o], mate))
        cb.wait()
        ys = lax.rem(y - o + NY, NY)
        last.append(send(wb.at[:, c, :, ys], wb.at[:, c, :, ys], gcb_s.at[o], gcb_r.at[o], mate))
    loads[2].wait()
    for cp in last:
        cp.wait()

    wa2, wb2 = wa.reshape(D, FF), wb.reshape(D, FF)

    def tile(i, _):
        r = pl.ds(pl.multiple_of(i * 256, 256), 256)
        gate = jnp.dot(nxt[r, :], wa2[...], preferred_element_type=f32)
        up = jnp.dot(nxt[r, :], wb2[...], preferred_element_type=f32)
        out_ref[r, :] = (gate / (1.0 + jnp.exp(-gate)) * up).astype(bf16)
        return 0

    lax.fori_loop(0, TOK // 256, tile, 0)


def shards(tokens, grad_out, master_weight, first_moment, second_moment, next_tokens):
    any_ = pl.BlockSpec(memory_space=pl.ANY)
    vm = pl.BlockSpec(memory_space=pltpu.VMEM)
    V = pltpu.VMEM
    dma = pltpu.SemaphoreType.DMA

    def pair(*shape):
        return [dma(shape), dma(shape)]

    scratch = [
        V((TOK, D), bf16), V((TOK, 2 * FF), bf16), V((TOK, D), bf16),
        V((NX, NZ, NY, ROWS, 2 * FF), f32), V((NX, NZ, NY, ROWS, 2 * FF), bf16), V((NX, NZ, NY, ROWS, 2 * FF), bf16),
        V((NX, NZ, NY, ROWS, FF), bf16), V((NY, NX, NZ, ROWS, FF), bf16),
        V((NX - 1, NZ, NY, ROWS, FF), bf16), V((NY - 1, NX, NZ, ROWS, FF), bf16),
        V((NY, NZ, ROWS, FF), bf16), V((NX, NZ, ROWS, FF), bf16),
        V((NY - 1, NZ, ROWS, FF), bf16), V((NX - 1, NZ, ROWS, FF), bf16),
        V((NZ, ROWS, 2 * FF), bf16), V((NZ - 1, ROWS, 2 * FF), bf16),
        V((4, 2, 128), f32), V((NZ - 1, 2, 128), f32), V((NY - 1, 2, 128), f32), V((NX - 1, 2, 128), f32), V((1, 2, 128), f32),
        V((ROWS, 2 * FF), bf16), V((NZ, ROWS, 2 * FF), bf16),
        V((NX, NC, NZ, NY, ROWS, FF), bf16), V((NX, NC, NZ, NY, ROWS, FF), bf16),
        dma((3,)),
        *pair(NX), *pair(NX - 1), *pair(NY - 1, NX), *pair(NY - 1), *pair(NX - 1), *pair(NZ - 1),
        *pair(NZ - 1), *pair(NY - 1), *pair(NX - 1), *pair(1),
        *pair(NZ - 1), *pair(NY - 1), *pair(NX - 1), *pair(NX - 1), *pair(NY - 1), *pair(NX), *pair(NY),
    ]
    return pl.pallas_call(
        body,
        out_shape=(
            jax.ShapeDtypeStruct((ROWS, 2 * FF), f32),
            jax.ShapeDtypeStruct((ROWS, 2 * FF), f32),
            jax.ShapeDtypeStruct((TOK, FF), bf16),
        ),
        in_specs=[any_, any_, vm, vm, vm, any_],
        out_specs=(vm, vm, vm),
        scratch_shapes=scratch,
        compiler_params=pltpu.CompilerParams(
            collective_id=0, has_side_effects=True, vmem_limit_bytes=60 * 1024 * 1024
        ),
    )(tokens, grad_out, master_weight, first_moment, second_moment, next_tokens)


def solution(mesh):
    split = Mesh(mesh.devices.reshape(NX, NC, NZ, NY), AXES)
    rows = P(AXES, None)
    return jax.shard_map(
        shards, mesh=split, in_specs=(rows,) * 6, out_specs=(rows,) * 3, check_vma=False
    )
```

```python
import math

import jax
import jax.numpy as jnp
from jax import lax
from jax.experimental import pallas as pl
from jax.experimental.pallas import tpu as pltpu
from jax.sharding import Mesh
from jax.sharding import PartitionSpec as P

NX, NC, NZ, NY = 4, 2, 8, 4
ROWS = 8
D = 2048
FF = 512
TOK = 1024
AXES = ("x", "c", "z", "y")
MESH = pl.DeviceIdType.MESH
FAR = (2, 1, 3)
FAR_Z = (4, 3, 5, 2, 6, 1, 7)
f32 = jnp.float32
bf16 = jnp.bfloat16


def body(
    tok_hbm, cot_hbm, w_hbm, m_hbm, v_hbm, nxt_hbm,
    nf_hbm, nv_hbm, out_hbm,
    tok, cot, nxt, pw, own, give, take,
    sa, sb, ra1, rb1, ta, tb, ra2, rb2, tz, rz, sqz, rsqz, rsq, gz, wa, wb, gate_acc, up_acc, nfv, out,
    ld_t, ld_n, ld, core_s, core_r, a1_s, a1_r, b1_s, b1_r, a2_s, a2_r, b2_s, b2_r, z_s, z_r,
    pw_s, pw_r, qz_s, qz_r, q_s, q_r, g_s, g_r,
    ga_s, ga_r, gb_s, gb_r, ha_s, ha_r, hb_s, hb_r, ca_s, ca_r, cb_s, cb_r, st,
):
    x, c, z, y = (lax.axis_index(a) for a in AXES)
    other = 1 - c

    def at_x(o):
        return lax.rem(x + o, NX)

    def at_y(o):
        return lax.rem(y + o, NY)

    def at_z(o):
        return lax.rem(z + o, NZ)

    def xp(o):
        return {"x": at_x(o)}

    def yp(o):
        return {"y": at_y(o)}

    def zp(o):
        return {"z": at_z(o)}

    mate = {"c": other}
    plane = [
        (ox, oc, oy) for ox in (2, 1, 3, 0) for oy in (2, 1, 3, 0) for oc in (1, 0) if ox or oc or oy
    ]

    def in_plane(ox, oc, oy):
        return {"x": at_x(ox), "c": other if oc else c, "y": at_y(oy)}

    sent = []

    def send(src, dst, ss, rs, to):
        cp = pltpu.make_async_remote_copy(
            src_ref=src, dst_ref=dst, send_sem=ss, recv_sem=rs, device_id=to, device_id_type=MESH
        )
        cp.start()
        sent.append(cp)
        return cp

    def arrived(dst, rs):
        pltpu.make_async_remote_copy(
            src_ref=dst, dst_ref=dst, send_sem=rs, recv_sem=rs, device_id=mate, device_id_type=MESH
        ).wait_recv()

    barrier = pltpu.get_barrier_semaphore()
    for o in plane:
        pl.semaphore_signal(barrier, inc=1, device_id=in_plane(*o), device_id_type=MESH)
    for o in FAR_Z:
        pl.semaphore_signal(barrier, inc=1, device_id=zp(o), device_id_type=MESH)

    offs = (2, 1, 3, 0)
    blocks = [at_x(o) for o in offs]
    load_cot = pltpu.make_async_copy(cot_hbm, cot, ld.at[0])
    load_tok = []
    for j in range(NX):
        for i, cc in enumerate((other, c)):
            start = pl.multiple_of(blocks[j] * 512 + cc * 256, 256)
            load_tok.append(
                pltpu.make_async_copy(tok_hbm.at[:, pl.ds(start, 256)], tok.at[2 * j + i], ld_t.at[2 * j + i])
            )
    load_pw = [
        pltpu.make_async_copy(h, pw.at[i, z], ld.at[1 + i]) for i, h in enumerate((w_hbm, m_hbm, v_hbm))
    ]
    load_nxt = [
        pltpu.make_async_copy(nxt_hbm.at[:, pl.ds(k * 512, 512)], nxt.at[k], ld_n.at[k]) for k in range(NX)
    ]
    for cp in [load_tok[0], load_cot, load_tok[1]]:
        cp.start()
    load_cot.wait()
    load_tok[0].wait()
    for cp in load_tok[2:] + load_pw:
        cp.start()

    def block_grad(i):
        if i:
            load_tok[i].wait()
        return lax.dot_general(tok[i], cot[...], (((0,), (0,)), ((), ())), preferred_element_type=f32)

    def pass_on(src, o, to):
        slot = at_z(NZ - src)
        return send(pw.at[:, slot], pw.at[:, slot], pw_s.at[o - 1], pw_r.at[o - 1], zp(to))

    def combine(j):
        xb, o = blocks[j], offs[j]
        core[j].wait_recv()
        total = own[j] + take[j].astype(f32)
        gate = total[:, :, :, :FF].astype(bf16)
        up = total[:, :, :, FF:].astype(bf16)
        for k in range(NY):
            sa[j, k] = gate[:, k]
            sb[k, xb] = up[:, k]
        for k in (2, 1, 3, 0):
            yk = at_y(k)
            if o:
                send(sa.at[j, yk], ra1.at[o - 1, k], a1_s.at[o - 1, k], a1_r.at[o - 1, k], xp(o))
            if k:
                send(sb.at[yk, xb], rb1.at[k - 1, j], b1_s.at[k - 1, j], b1_r.at[k - 1, j], yp(k))

    core = []
    for j in range(NX):
        give[j] = block_grad(2 * j).astype(bf16).reshape(NZ, NY, ROWS, 2 * FF)
        if j == 0:
            pl.semaphore_wait(barrier, len(plane) + len(FAR_Z))
        core.append(send(give.at[j], take.at[j], core_s.at[j], core_r.at[j], mate))
        own[j] = block_grad(2 * j + 1).reshape(NZ, NY, ROWS, 2 * FF)
        if j == 0:
            for cp in load_pw:
                cp.wait()
            pass_on(0, 4, 4)
            pass_on(0, 1, 1)
            pass_on(0, 7, 7)
        else:
            combine(j - 1)
    combine(NX - 1)
    for cp in load_nxt:
        cp.start()


    def second_b(j):
        total = sb[y, blocks[j]].astype(f32)
        for k in range(1, NY):
            arrived(rb1.at[k - 1, j], b1_r.at[k - 1, j])
            total += rb1[k - 1, j].astype(f32)
        tb[j] = total.astype(bf16)
        o = offs[j]
        if o:
            send(tb.at[j], rb2.at[o - 1], b2_s.at[o - 1], b2_r.at[o - 1], xp(o))

    def second_a(k):
        total = sa[NX - 1, at_y(k)].astype(f32)
        for o in range(1, NX):
            arrived(ra1.at[o - 1, k], a1_r.at[o - 1, k])
            total += ra1[o - 1, k].astype(f32)
        ta[k] = total.astype(bf16)
        if k:
            send(ta.at[k], ra2.at[k - 1], a2_s.at[k - 1], a2_r.at[k - 1], yp(k))

    for j in range(NX - 1):
        second_b(j)
    arrived(pw.at[:, at_z(7)], pw_r.at[0])
    pass_on(1, 2, 1)
    arrived(pw.at[:, at_z(1)], pw_r.at[6])
    pass_on(7, 6, 7)
    for k in (2, 1, 3):
        second_a(k)
    second_b(NX - 1)
    second_a(0)

    arrived(pw.at[:, at_z(6)], pw_r.at[1])
    pass_on(2, 3, 1)
    arrived(pw.at[:, at_z(2)], pw_r.at[5])
    pass_on(6, 5, 7)
    total = ta[0].astype(f32)
    for k in range(1, NY):
        arrived(ra2.at[k - 1], a2_r.at[k - 1])
        total += ra2[k - 1].astype(f32)
    tz[:, :, :FF] = total.astype(bf16)
    total = tb[NX - 1].astype(f32)
    for k in range(1, NX):
        arrived(rb2.at[k - 1], b2_r.at[k - 1])
        total += rb2[k - 1].astype(f32)
    tz[:, :, FF:] = total.astype(bf16)

    for o in FAR_Z:
        send(tz.at[at_z(o)], rz.at[o - 1], z_s.at[o - 1], z_r.at[o - 1], zp(o))
    grad = tz[z].astype(f32)
    for o in (1, 7, 2, 6, 3, 5, 4):
        arrived(rz.at[o - 1], z_r.at[o - 1])
        grad += rz[o - 1].astype(f32)

    def fold(t):
        t = t * t
        t = jnp.sum(t, axis=0, keepdims=True)
        return t[:, 0:128] + t[:, 128:256] + t[:, 256:384] + t[:, 384:512]

    sqz[...] = jnp.concatenate([fold(grad[:, :FF]), fold(grad[:, FF:])], axis=0)
    for o in FAR_Z:
        send(sqz, rsqz.at[o - 1], qz_s.at[o - 1], qz_r.at[o - 1], zp(o))
    gz[z] = grad.astype(bf16)
    both = sqz[...]
    for o in (1, 7, 2, 6, 3, 5, 4):
        arrived(rsqz.at[o - 1], qz_r.at[o - 1])
        both += rsqz[o - 1]
    rsq[0] = both
    slots = {o: (o[0] * NC + o[1]) * NY + o[2] for o in plane}
    for o in plane:
        k = slots[o]
        send(rsq.at[0], rsq.at[k], q_s.at[k], q_r.at[k], in_plane(*o))
    for o in FAR_Z:
        send(gz.at[z], gz.at[z], g_s.at[o - 1], g_r.at[o - 1], zp(o))
    for o in (1, 7, 2, 6, 3, 5, 4):
        arrived(gz.at[at_z(NZ - o)], g_r.at[o - 1])
    for o in (3, 5, 4):
        arrived(pw.at[:, at_z(NZ - o)], pw_r.at[o - 1])
    for o in plane[::-1]:
        arrived(rsq.at[slots[o]], q_r.at[slots[o]])
    both = jnp.sum(rsq[...], axis=0)
    limit = math.sqrt(D * FF)
    factor = jnp.minimum(1.0, limit / jnp.sqrt(jnp.sum(both, axis=1, keepdims=True) + 1e-06))
    gate_factor, up_factor = factor[0:1], factor[1:2]
    first_scale = 0.003 / (1.0 - 0.9**10)
    second_scale = 1.0 / (1.0 - 0.95**10)

    def moments(g, slot):
        clipped = jnp.concatenate([g[:, :FF] * gate_factor, g[:, FF:] * up_factor], axis=1)
        return 0.9 * pw[1, slot] + 0.1 * clipped, 0.95 * pw[2, slot] + 0.05 * clipped * clipped

    for k in range(NZ):
        first, second = moments(gz[k].astype(f32), k)
        low = pw[0, k] * (1.0 - 0.003 * 0.1) - (first * first_scale) / (jnp.sqrt(second * second_scale) + 1e-08)
        low = low.astype(bf16)
        wa[x, c, k, y] = low[:, :FF]
        wb[x, c, k, y] = low[:, FF:]

    def pa(ox, oy, lo=0, n=NZ):
        return wa.at[at_x(NX - ox), c, pl.ds(lo, n), at_y(NY - oy)]

    def pb(ox, oy, lo=0, n=NZ):
        return wb.at[at_x(NX - ox), c, pl.ds(lo, n), at_y(NY - oy)]

    def to_mate(piece, ox, oy, ss, rs):
        send(piece(ox, oy), piece(ox, oy), ss.at[ox, oy], rs.at[ox, oy], mate)

    def spread_a(oy):
        for o in (1, 3):
            send(pa(0, oy), pa(0, oy), ga_s.at[o, oy], ga_r.at[o, oy], xp(o))
        to_mate(pa, 0, oy, ca_s, ca_r)

    def spread_b(ox):
        for o in (1, 3):
            send(pb(ox, 0), pb(ox, 0), gb_s.at[ox, o], gb_r.at[ox, o], yp(o))
        to_mate(pb, ox, 0, cb_s, cb_r)

    for o in (1, 3, 2):
        send(pa(0, 0), pa(0, 0), ga_s.at[0, o], ga_r.at[0, o], yp(o))
        send(pb(0, 0), pb(0, 0), gb_s.at[o, 0], gb_r.at[o, 0], xp(o))
    spread_a(0)
    spread_b(0)

    first, second = moments(grad, z)
    nfv[0] = first
    nfv[1] = second
    stores = [pltpu.make_async_copy(nfv.at[i], h, st.at[i]) for i, h in enumerate((nf_hbm, nv_hbm))]
    for cp in stores:
        cp.start()

    half = NZ // 2

    def forward(o):
        arrived(pa(0, o), ga_r.at[0, o])
        spread_a(o)
        arrived(pb(o, 0), gb_r.at[o, 0])
        spread_b(o)

    def relay(k):
        for i, o in enumerate((1, 3)):
            arrived(pa(o, k), ga_r.at[o, k])
            part = pa(o, k, i * half, half)
            send(part, part, ha_s.at[i, k], ha_r.at[i, k], xp(o))
            to_mate(pa, o, k, ca_s, ca_r)
            arrived(pb(k, o), gb_r.at[k, o])
            part = pb(k, o, i * half, half)
            send(part, part, hb_s.at[i, k], hb_r.at[i, k], yp(o))
            to_mate(pb, k, o, cb_s, cb_r)

    def last(k):
        for i in range(2):
            arrived(pa(2, k, i * half, half), ha_r.at[i, k])
            arrived(pb(k, 2, i * half, half), hb_r.at[i, k])
        to_mate(pa, 2, k, ca_s, ca_r)
        to_mate(pb, k, 2, cb_s, cb_r)

    wa_k, wb_k = wa.reshape(NX, 512, FF), wb.reshape(NX, 512, FF)
    theirs_a = wa.at[:, other]
    theirs_b = wb.at[:, other]

    def mate_a(ox):
        for oy in range(NY):
            arrived(theirs_a.at[at_x(NX - ox), :, at_y(NY - oy)], ca_r.at[ox, oy])

    def mate_b(ox):
        for oy in range(NY):
            arrived(theirs_b.at[at_x(NX - ox), :, at_y(NY - oy)], cb_r.at[ox, oy])

    def start_of(acc, w_k):
        k = x

        def tile(i, _):
            r = pl.ds(pl.multiple_of(i * 256, 256), 256)
            acc[r, :] = jnp.dot(nxt[k, r, :], w_k[k], preferred_element_type=f32)
            return 0

        lax.fori_loop(0, TOK // 256, tile, 0)

    def rest():
        ks = [at_x(NX - ox) for ox in (1, 3, 2)]

        def store(i):
            r = pl.ds(pl.multiple_of(i * 256, 256), 256)
            return pltpu.make_async_copy(out.at[r], out_hbm.at[r], st.at[2 + i])

        def tile(i, _):
            r = pl.ds(pl.multiple_of(i * 256, 256), 256)
            gate, up = gate_acc[r, :], up_acc[r, :]
            for k in ks:
                gate += jnp.dot(nxt[k, r, :], wa_k[k], preferred_element_type=f32)
            for k in ks:
                up += jnp.dot(nxt[k, r, :], wb_k[k], preferred_element_type=f32)
            out[r, :] = (gate / (1.0 + jnp.exp(-gate)) * up).astype(bf16)
            store(i).start()
            return 0

        lax.fori_loop(0, TOK // 256, tile, 0)
        stores.extend(store(i) for i in range(TOK // 256))

    forward(1)
    forward(3)
    relay(0)
    forward(2)
    for cp in load_nxt:
        cp.wait()
    relay(1)
    relay(3)
    mate_a(0)
    start_of(gate_acc, wa_k)
    last(0)
    relay(2)
    mate_b(0)
    start_of(up_acc, wb_k)
    last(1)
    last(3)
    last(2)
    for ox in (1, 3, 2):
        mate_a(ox)
        mate_b(ox)
    rest()
    for cp in sent:
        cp.wait_send()
    for cp in stores:
        cp.wait()


def keep(a_ref, b_ref, c_ref, a_out, b_out, c_out, a_buf, b_buf, c_buf, in_sem, out_sem):
    part = TOK // 4
    moves = [(c_ref.at[pl.ds(i * part, part)], c_buf.at[i], c_out.at[pl.ds(i * part, part)]) for i in range(4)]
    moves += [(a_ref, a_buf, a_out), (b_ref, b_buf, b_out)]
    reads = [pltpu.make_async_copy(s, t, in_sem.at[i]) for i, (s, t, _) in enumerate(moves)]
    writes = [pltpu.make_async_copy(t, d, out_sem.at[i]) for i, (_, t, d) in enumerate(moves)]
    for cp in reads:
        cp.start()
    for r, w in zip(reads, writes):
        r.wait()
        w.start()
    for cp in writes:
        cp.wait()


def shards(tokens, grad_out, master_weight, first_moment, second_moment, next_tokens):
    any_ = pl.BlockSpec(memory_space=pltpu.HBM)
    V = pltpu.VMEM
    dma = pltpu.SemaphoreType.DMA

    def pair(*shape):
        return [dma(shape), dma(shape)]

    block = (NX, NZ, NY, ROWS, 2 * FF)
    scratch = [
        V((2 * NX, TOK, 256), bf16), V((TOK, 2 * FF), bf16), V((NX, TOK, 512), bf16), V((3, NZ, ROWS, 2 * FF), f32),
        V(block, f32), V(block, bf16), V(block, bf16),
        V((NX, NY, NZ, ROWS, FF), bf16), V((NY, NX, NZ, ROWS, FF), bf16),
        V((NX - 1, NY, NZ, ROWS, FF), bf16), V((NY - 1, NX, NZ, ROWS, FF), bf16),
        V((NY, NZ, ROWS, FF), bf16), V((NX, NZ, ROWS, FF), bf16),
        V((NY - 1, NZ, ROWS, FF), bf16), V((NX - 1, NZ, ROWS, FF), bf16),
        V((NZ, ROWS, 2 * FF), bf16), V((NZ - 1, ROWS, 2 * FF), bf16),
        V((2, 128), f32), V((NZ - 1, 2, 128), f32), V((NX * NC * NY, 2, 128), f32),
        V((NZ, ROWS, 2 * FF), bf16),
        V((NX, NC, NZ, NY, ROWS, FF), bf16), V((NX, NC, NZ, NY, ROWS, FF), bf16),
        V((TOK, FF), f32), V((TOK, FF), f32), V((2, ROWS, 2 * FF), f32), V((TOK, FF), bf16),
        dma((2 * NX,)), dma((NX,)), dma((4,)),
        *pair(NX), *pair(NX - 1, NY), *pair(NY - 1, NX), *pair(NY - 1), *pair(NX - 1), *pair(NZ - 1),
        *pair(NZ - 1), *pair(NZ - 1), *pair(NX * NC * NY), *pair(NZ - 1),
        *pair(NX, NY), *pair(NX, NY), *pair(2, NY), *pair(2, NX), *pair(NX, NY), *pair(NX, NY), dma((6,)),
    ]
    shapes = (
        jax.ShapeDtypeStruct((ROWS, 2 * FF), f32),
        jax.ShapeDtypeStruct((ROWS, 2 * FF), f32),
        jax.ShapeDtypeStruct((TOK, FF), bf16),
    )
    results = pl.pallas_call(
        body,
        out_shape=shapes,
        in_specs=[any_] * 6,
        out_specs=(any_,) * 3,
        scratch_shapes=scratch,
        compiler_params=pltpu.CompilerParams(
            collective_id=0, has_side_effects=True, vmem_limit_bytes=60 * 1024 * 1024
        ),
    )(tokens, grad_out, master_weight, first_moment, second_moment, next_tokens)
    return pl.pallas_call(
        keep,
        out_shape=shapes,
        in_specs=[any_] * 3,
        out_specs=(any_,) * 3,
        scratch_shapes=[
            V((ROWS, 2 * FF), f32), V((ROWS, 2 * FF), f32), V((4, TOK // 4, FF), bf16), *pair(6),
        ],
        compiler_params=pltpu.CompilerParams(vmem_limit_bytes=60 * 1024 * 1024),
    )(*results)


def solution(mesh):
    split = Mesh(mesh.devices.reshape(NX, NC, NZ, NY), AXES)
    rows = P(AXES, None)
    return jax.shard_map(
        shards, mesh=split, in_specs=(rows,) * 6, out_specs=(rows,) * 3, check_vma=False
    )
```

```python
import math

import jax
import jax.numpy as jnp
from jax import lax
from jax.experimental import pallas as pl
from jax.experimental.pallas import tpu as pltpu
from jax.sharding import Mesh
from jax.sharding import PartitionSpec as P

NX, NC, NZ, NY = 4, 2, 8, 4
ROWS = 8
D = 2048
FF = 512
TOK = 1024
AXES = ("x", "c", "z", "y")
MESH = pl.DeviceIdType.MESH
FAR_Z = (4, 3, 5, 2, 6, 1, 7)
f32 = jnp.float32
bf16 = jnp.bfloat16


def body(
    tok_hbm, cot_hbm, w_hbm, m_hbm, v_hbm, nxt_hbm,
    nf_hbm, nv_hbm, out_hbm,
    tok, cot, nxt, pw, own, give, take,
    sa, sb, fa, fb, ra1, rb1, ta, tb, ra2, rb2, tz, rz, sqz, rsqz, rsq, gz, wa, wb, gate_acc, up_acc, nfv, out,
    ld_t, ld_n, ld, st, done, core_r, fa_r, fb_r, a1_r, b1_r, a2_r, b2_r, z_r, pw_r, qz_r, q_r, g_r,
    ga_r, gb_r, na_r, nb_r, ha_r, hb_r, ca_r, cb_r,
):
    x, c, z, y = (lax.axis_index(a) for a in AXES)
    other = 1 - c

    def at_x(o):
        return lax.rem(x + o, NX)

    def at_y(o):
        return lax.rem(y + o, NY)

    def at_z(o):
        return lax.rem(z + o, NZ)

    def xp(o):
        return {"x": at_x(o)}

    def yp(o):
        return {"y": at_y(o)}

    def zp(o):
        return {"z": at_z(o)}

    mate = {"c": other}
    plane = [
        (ox, oc, oy) for ox in (2, 1, 3, 0) for oy in (2, 1, 3, 0) for oc in (1, 0) if ox or oc or oy
    ]

    def in_plane(ox, oc, oy):
        return {"x": at_x(ox), "c": other if oc else c, "y": at_y(oy)}

    CORE, A1, B1, A2, B2, Z, PW, QZ, Q, G, GA, GB, CA, CB = range(14)

    def send(src, dst, kind, rs, to):
        pltpu.make_async_remote_copy(
            src_ref=src, dst_ref=dst, send_sem=done.at[kind], recv_sem=rs, device_id=to, device_id_type=MESH
        ).start()

    def handle(ref, sem):
        return pltpu.make_async_remote_copy(
            src_ref=ref, dst_ref=ref, send_sem=sem, recv_sem=sem, device_id=mate, device_id_type=MESH
        )

    def arrived(dst, rs):
        handle(dst, rs).wait_recv()

    barrier = pltpu.get_barrier_semaphore()
    for o in plane:
        pl.semaphore_signal(barrier, inc=1, device_id=in_plane(*o), device_id_type=MESH)
    for o in FAR_Z:
        pl.semaphore_signal(barrier, inc=1, device_id=zp(o), device_id_type=MESH)

    offs = (2, 1, 3, 0)
    blocks = [at_x(o) for o in offs]
    load_cot = pltpu.make_async_copy(cot_hbm, cot, ld.at[0])
    load_tok = []
    for j in range(NX):
        for i, cc in enumerate((other, c)):
            start = pl.multiple_of(blocks[j] * 512 + cc * 256, 256)
            load_tok.append(
                pltpu.make_async_copy(tok_hbm.at[:, pl.ds(start, 256)], tok.at[2 * j + i], ld_t.at[2 * j + i])
            )
    load_pw = [
        pltpu.make_async_copy(h, pw.at[i, z], ld.at[1 + i]) for i, h in enumerate((w_hbm, m_hbm, v_hbm))
    ]
    load_nxt = [
        pltpu.make_async_copy(nxt_hbm.at[:, pl.ds(k * 512, 512)], nxt.at[k], ld_n.at[k]) for k in range(NX)
    ]
    for cp in [load_tok[0], load_cot, load_tok[1]]:
        cp.start()
    load_cot.wait()
    load_tok[0].wait()
    for cp in load_tok[2:] + load_pw:
        cp.start()

    def block_grad(i):
        if i:
            load_tok[i].wait()
        return lax.dot_general(tok[i], cot[...], (((0,), (0,)), ((), ())), preferred_element_type=f32)

    def pass_on(src, o, to):
        slot = at_z(NZ - src)
        send(pw.at[:, slot], pw.at[:, slot], PW, pw_r.at[o - 1], zp(to))

    half = NZ // 2
    lower, upper = pl.ds(0, half), pl.ds(half, half)
    whole = pl.ds(0, NZ)
    via_next, via_prev = (2, 0), (1, 3)

    def gate_sum(j, k, zs=whole):
        yk = at_y(k)
        return own[j, zs, yk, :, pl.ds(0, FF)] + take[j, zs, yk, :, pl.ds(0, FF)].astype(f32)

    def up_sum(j, k, zs=whole):
        yk = at_y(k)
        return own[j, zs, yk, :, pl.ds(FF, FF)] + take[j, zs, yk, :, pl.ds(FF, FF)].astype(f32)

    def near_a(j, k, value):
        sa[j, k] = value.astype(bf16)
        send(sa.at[j, k], ra1.at[k, j - 1], A1, a1_r.at[k], xp(1 if j == 1 else 3))

    def near_b(j, i, zs, value):
        sb[j, 1 + i, zs] = value.astype(bf16)
        send(sb.at[j, 1 + i, zs], rb1.at[j, i, zs], B1, b1_r.at[j], yp((1, 3)[i]))

    def combine(j):
        arrived(take.at[j], core_r.at[j])
        if j == 0:
            for k in (2, 1, 0, 3):
                sa[0, k] = gate_sum(0, k).astype(bf16)
                i, n = (0, via_next.index(k)) if k in via_next else (1, via_prev.index(k))
                send(sa.at[0, k], fa.at[i, n], A1, fa_r.at[i], xp(1 if i == 0 else 3))
        sb[j, 0] = up_sum(j, 2).astype(bf16)
        for zs, o in ((lower, 1), (upper, 3)):
            send(sb.at[j, 0, zs], fb.at[j, zs], B1, fb_r.at[j], yp(o))
        near_b(j, 0, upper, up_sum(j, 1, upper))
        near_b(j, 1, lower, up_sum(j, 3, lower))
        if j == 1:
            for k in via_prev:
                near_a(1, k, gate_sum(1, k))
        if j == 2:
            for k in via_next:
                near_a(2, k, gate_sum(2, k))

    def add_a(i):
        arrived(fa.at[i], fa_r.at[i])
        for n, k in enumerate((via_next, via_prev)[i]):
            near_a(1 + i, k, gate_sum(1 + i, k) + fa[i, n].astype(f32))

    def add_b(j):
        arrived(fb.at[j], fb_r.at[j])
        near_b(j, 0, lower, up_sum(j, 1, lower) + fb[j, lower].astype(f32))
        near_b(j, 1, upper, up_sum(j, 3, upper) + fb[j, upper].astype(f32))

    def second_a(k):
        total = gate_sum(NX - 1, k)
        arrived(ra1.at[k], a1_r.at[k])
        total += ra1[k, 0].astype(f32) + ra1[k, 1].astype(f32)
        if k:
            ta[k - 1] = total.astype(bf16)
            send(ta.at[k - 1], ra2.at[k - 1], A2, a2_r.at[0], yp(k))
        return total

    def second_b(j):
        total = up_sum(j, 0)
        arrived(rb1.at[j], b1_r.at[j])
        total += rb1[j, 0].astype(f32) + rb1[j, 1].astype(f32)
        o = offs[j]
        if o:
            tb[o - 1] = total.astype(bf16)
            send(tb.at[o - 1], rb2.at[o - 1], B2, b2_r.at[0], xp(o))
        return total

    for j in range(NX):
        give[j] = block_grad(2 * j).astype(bf16).reshape(NZ, NY, ROWS, 2 * FF)
        if j == 0:
            pl.semaphore_wait(barrier, len(plane) + len(FAR_Z))
        send(give.at[j], take.at[j], CORE, core_r.at[j], mate)
        own[j] = block_grad(2 * j + 1).reshape(NZ, NY, ROWS, 2 * FF)
        if j == 0:
            for cp in load_pw:
                cp.wait()
            pass_on(0, 4, 4)
            pass_on(0, 1, 1)
            pass_on(0, 7, 7)
        else:
            combine(j - 1)
    combine(NX - 1)
    for cp in load_nxt:
        cp.start()
    add_a(0)
    add_b(0)
    add_a(1)
    add_b(1)
    add_b(2)
    add_b(3)
    second_b(0)
    arrived(pw.at[:, at_z(7)], pw_r.at[0])
    pass_on(1, 2, 1)
    arrived(pw.at[:, at_z(1)], pw_r.at[6])
    pass_on(7, 6, 7)
    second_a(2)
    second_a(1)
    second_b(1)
    second_b(2)
    second_a(3)
    total = second_a(0)
    arrived(ra2, a2_r.at[0])
    for k in range(NY - 1):
        total += ra2[k].astype(f32)
    tz[:, :, :FF] = total.astype(bf16)
    total = second_b(NX - 1)
    arrived(rb2, b2_r.at[0])
    for k in range(NX - 1):
        total += rb2[k].astype(f32)
    tz[:, :, FF:] = total.astype(bf16)

    for o in FAR_Z:
        send(tz.at[at_z(o)], rz.at[o - 1], Z, z_r.at[0], zp(o))
    arrived(pw.at[:, at_z(6)], pw_r.at[1])
    pass_on(2, 3, 1)
    arrived(pw.at[:, at_z(2)], pw_r.at[5])
    pass_on(6, 5, 7)
    grad = tz[z].astype(f32)
    arrived(rz, z_r.at[0])
    for o in range(NZ - 1):
        grad += rz[o].astype(f32)

    def fold(t):
        t = t * t
        t = jnp.sum(t, axis=0, keepdims=True)
        return t[:, 0:128] + t[:, 128:256] + t[:, 256:384] + t[:, 384:512]

    sqz[...] = jnp.concatenate([fold(grad[:, :FF]), fold(grad[:, FF:])], axis=0)
    for o in FAR_Z:
        send(sqz, rsqz.at[o - 1], QZ, qz_r.at[0], zp(o))
    gz[0] = grad.astype(bf16)
    both = sqz[...]
    arrived(rsqz, qz_r.at[0])
    for o in range(NZ - 1):
        both += rsqz[o]
    rsq[0] = both
    for i, o in enumerate(plane):
        send(rsq.at[0], rsq.at[1 + i], Q, q_r.at[0], in_plane(*o))
    for o in FAR_Z:
        send(gz.at[0], gz.at[o], G, g_r.at[0], zp(o))
    arrived(gz.at[pl.ds(1, NZ - 1)], g_r.at[0])
    for o in (3, 5, 4):
        arrived(pw.at[:, at_z(NZ - o)], pw_r.at[o - 1])
    arrived(rsq.at[pl.ds(1, len(plane))], q_r.at[0])
    both = jnp.sum(rsq[...], axis=0)
    limit = math.sqrt(D * FF)
    factor = jnp.minimum(1.0, limit / jnp.sqrt(jnp.sum(both, axis=1, keepdims=True) + 1e-06))
    gate_factor, up_factor = factor[0:1], factor[1:2]
    first_scale = 0.003 / (1.0 - 0.9**10)
    second_scale = 1.0 / (1.0 - 0.95**10)

    def moments(g, slot):
        clipped = jnp.concatenate([g[:, :FF] * gate_factor, g[:, FF:] * up_factor], axis=1)
        return 0.9 * pw[1, slot] + 0.1 * clipped, 0.95 * pw[2, slot] + 0.05 * clipped * clipped

    for o in range(NZ):
        k = at_z(NZ - o)
        first, second = moments(gz[o].astype(f32), k)
        low = pw[0, k] * (1.0 - 0.003 * 0.1) - (first * first_scale) / (jnp.sqrt(second * second_scale) + 1e-08)
        low = low.astype(bf16)
        wa[x, c, k, y] = low[:, :FF]
        wb[x, c, k, y] = low[:, FF:]

    def pa(ox, oy, lo=0, n=NZ):
        return wa.at[at_x(NX - ox), c, pl.ds(lo, n), at_y(NY - oy)]

    def pb(ox, oy, lo=0, n=NZ):
        return wb.at[at_x(NX - ox), c, pl.ds(lo, n), at_y(NY - oy)]

    def to_mate_a(ox, oy):
        send(pa(ox, oy), pa(ox, oy), CA, ca_r.at[ox], mate)

    def to_mate_b(ox, oy):
        send(pb(ox, oy), pb(ox, oy), CB, cb_r.at[ox], mate)

    def spread_a(oy):
        for i, o in enumerate((1, 3)):
            send(pa(0, oy), pa(0, oy), GA, na_r.at[i, oy], xp(o))
        to_mate_a(0, oy)

    def spread_b(ox):
        for i, o in enumerate((1, 3)):
            send(pb(ox, 0), pb(ox, 0), GB, nb_r.at[i, ox], yp(o))
        to_mate_b(ox, 0)

    for o in (1, 3, 2):
        send(pa(0, 0), pa(0, 0), GA, ga_r.at[o - 1], yp(o))
        send(pb(0, 0), pb(0, 0), GB, gb_r.at[o - 1], xp(o))
    spread_a(0)
    spread_b(0)

    first, second = moments(grad, z)
    nfv[0] = first
    nfv[1] = second
    stores = [pltpu.make_async_copy(nfv.at[i], h, st.at[i]) for i, h in enumerate((nf_hbm, nv_hbm))]
    for cp in stores:
        cp.start()

    def forward(o):
        arrived(pa(0, o), ga_r.at[o - 1])
        spread_a(o)
        arrived(pb(o, 0), gb_r.at[o - 1])
        spread_b(o)

    def relay(k):
        for i, o in enumerate((1, 3)):
            arrived(pa(o, k), na_r.at[i, k])
            part = pa(o, k, i * half, half)
            send(part, part, GA, ha_r.at[k], xp(o))
            to_mate_a(o, k)
            arrived(pb(k, o), nb_r.at[i, k])
            part = pb(k, o, i * half, half)
            send(part, part, GB, hb_r.at[k], yp(o))
            to_mate_b(k, o)

    def last(k):
        arrived(pa(2, k), ha_r.at[k])
        to_mate_a(2, k)
        arrived(pb(k, 2), hb_r.at[k])
        to_mate_b(k, 2)

    wa_k, wb_k = wa.reshape(NX, 512, FF), wb.reshape(NX, 512, FF)
    def mate_a(ox):
        arrived(wa.at[at_x(NX - ox), other], ca_r.at[ox])

    def mate_b(ox):
        arrived(wb.at[at_x(NX - ox), other], cb_r.at[ox])

    def start_of(acc, w_k):
        k = x

        def tile(i, _):
            r = pl.ds(pl.multiple_of(i * 256, 256), 256)
            acc[r, :] = jnp.dot(nxt[k, r, :], w_k[k], preferred_element_type=f32)
            return 0

        lax.fori_loop(0, TOK // 256, tile, 0)

    def rest():
        ks = [at_x(NX - ox) for ox in (1, 3, 2)]

        def store(i):
            r = pl.ds(pl.multiple_of(i * 256, 256), 256)
            return pltpu.make_async_copy(out.at[r], out_hbm.at[r], st.at[2 + i])

        def tile(i, _):
            r = pl.ds(pl.multiple_of(i * 256, 256), 256)
            gate, up = gate_acc[r, :], up_acc[r, :]
            for k in ks:
                gate += jnp.dot(nxt[k, r, :], wa_k[k], preferred_element_type=f32)
            for k in ks:
                up += jnp.dot(nxt[k, r, :], wb_k[k], preferred_element_type=f32)
            out[r, :] = (gate / (1.0 + jnp.exp(-gate)) * up).astype(bf16)
            store(i).start()
            return 0

        lax.fori_loop(0, TOK // 256, tile, 0)
        stores.extend(store(i) for i in range(TOK // 256))

    forward(1)
    forward(3)
    relay(0)
    forward(2)
    for cp in load_nxt:
        cp.wait()
    relay(1)
    relay(3)
    relay(2)
    last(0)
    mate_a(0)
    start_of(gate_acc, wa_k)
    last(1)
    last(3)
    mate_b(0)
    start_of(up_acc, wb_k)
    last(2)
    for ox in (1, 3, 2):
        mate_a(ox)
        mate_b(ox)
    rest()
    rows64 = pl.ds(0, 15 * 64)
    bytes_of = {
        CORE: give, A1: sa, B1: sb, A2: ta, B2: tb, Z: tz.at[pl.ds(0, NZ - 1)], PW: pw.at[:, pl.ds(0, NZ - 1)],
        QZ: rsqz, Q: rsq.at[pl.ds(1, len(plane))], G: gz.at[pl.ds(1, NZ - 1)],
        GA: wa.reshape(D, FF).at[rows64], GB: wb.reshape(D, FF).at[rows64], CA: wa.at[:, c], CB: wb.at[:, c],
    }
    for kind, ref in bytes_of.items():
        handle(ref, done.at[kind]).wait_send()
    for cp in stores:
        cp.wait()


def keep(a_ref, b_ref, c_ref, a_out, b_out, c_out, a_buf, b_buf, c_buf, in_sem, out_sem):
    part = TOK // 4
    moves = [(c_ref.at[pl.ds(i * part, part)], c_buf.at[i], c_out.at[pl.ds(i * part, part)]) for i in range(4)]
    moves += [(a_ref, a_buf, a_out), (b_ref, b_buf, b_out)]
    reads = [pltpu.make_async_copy(s, t, in_sem.at[i]) for i, (s, t, _) in enumerate(moves)]
    writes = [pltpu.make_async_copy(t, d, out_sem.at[i]) for i, (_, t, d) in enumerate(moves)]
    for cp in reads:
        cp.start()
    for r, w in zip(reads, writes):
        r.wait()
        w.start()
    for cp in writes:
        cp.wait()


def shards(tokens, grad_out, master_weight, first_moment, second_moment, next_tokens):
    any_ = pl.BlockSpec(memory_space=pltpu.HBM)
    V = pltpu.VMEM
    dma = pltpu.SemaphoreType.DMA

    block = (NX, NZ, NY, ROWS, 2 * FF)
    piece = (NZ, ROWS, FF)
    scratch = [
        V((2 * NX, TOK, 256), bf16), V((TOK, 2 * FF), bf16), V((NX, TOK, 512), bf16), V((3, NZ, ROWS, 2 * FF), f32),
        V(block, f32), V(block, bf16), V(block, bf16),
        V((NX - 1, NY, *piece), bf16), V((NX, NY - 1, *piece), bf16), V((2, 2, *piece), bf16), V((NX, *piece), bf16),
        V((NY, 2, *piece), bf16), V((NX, 2, *piece), bf16),
        V((NY - 1, *piece), bf16), V((NX - 1, *piece), bf16), V((NY - 1, *piece), bf16), V((NX - 1, *piece), bf16),
        V((NZ, ROWS, 2 * FF), bf16), V((NZ - 1, ROWS, 2 * FF), bf16),
        V((2, 128), f32), V((NZ - 1, 2, 128), f32), V((NX * NC * NY, 2, 128), f32),
        V((NZ, ROWS, 2 * FF), bf16),
        V((NX, NC, NZ, NY, ROWS, FF), bf16), V((NX, NC, NZ, NY, ROWS, FF), bf16),
        V((TOK, FF), f32), V((TOK, FF), f32), V((2, ROWS, 2 * FF), f32), V((TOK, FF), bf16),
        dma((2 * NX,)), dma((NX,)), dma((4,)), dma((6,)), dma((14,)),
        dma((NX,)), dma((2,)), dma((NX,)), dma((NY,)), dma((NX,)), dma((1,)), dma((1,)), dma((1,)),
        dma((NZ - 1,)), dma((1,)), dma((1,)), dma((1,)),
        dma((NY - 1,)), dma((NX - 1,)), dma((2, NY)), dma((2, NX)), dma((NY,)), dma((NX,)), dma((NX,)), dma((NX,)),
    ]
    shapes = (
        jax.ShapeDtypeStruct((ROWS, 2 * FF), f32),
        jax.ShapeDtypeStruct((ROWS, 2 * FF), f32),
        jax.ShapeDtypeStruct((TOK, FF), bf16),
    )
    results = pl.pallas_call(
        body,
        out_shape=shapes,
        in_specs=[any_] * 6,
        out_specs=(any_,) * 3,
        scratch_shapes=scratch,
        compiler_params=pltpu.CompilerParams(
            collective_id=0, has_side_effects=True, vmem_limit_bytes=60 * 1024 * 1024
        ),
    )(tokens, grad_out, master_weight, first_moment, second_moment, next_tokens)
    return pl.pallas_call(
        keep,
        out_shape=shapes,
        in_specs=[any_] * 3,
        out_specs=(any_,) * 3,
        scratch_shapes=[
            V((ROWS, 2 * FF), f32), V((ROWS, 2 * FF), f32), V((4, TOK // 4, FF), bf16),
            dma((6,)), dma((6,)),
        ],
        compiler_params=pltpu.CompilerParams(vmem_limit_bytes=60 * 1024 * 1024),
    )(*results)


def solution(mesh):
    split = Mesh(mesh.devices.reshape(NX, NC, NZ, NY), AXES)
    rows = P(AXES, None)
    return jax.shard_map(
        shards, mesh=split, in_specs=(rows,) * 6, out_specs=(rows,) * 3, check_vma=False
    )
```

```python
import math

import jax
import jax.numpy as jnp
from jax import lax
from jax.experimental import pallas as pl
from jax.experimental.pallas import tpu as pltpu
from jax.sharding import Mesh
from jax.sharding import PartitionSpec as P

NX, NC, NZ, NY = 4, 2, 8, 4
ROWS = 8
D = 2048
FF = 512
TOK = 1024
AXES = ("x", "c", "z", "y")
MESH = pl.DeviceIdType.MESH
FAR_Z = (4, 3, 5, 2, 6, 1, 7)
f32 = jnp.float32
bf16 = jnp.bfloat16


def body(
    tok_hbm, cot_hbm, w_hbm, m_hbm, v_hbm, nxt_hbm,
    nf_ref, nv_ref, out_ref,
    tok, cot, nxt, pw, own, give, take,
    sa, sb, fa, fb, ra1, rb1, ta, tb, ra2, rb2, tz, rz, sqz, rsqz, rsq, gz, wa, wb, gate_acc, up_acc,
    ld_t, ld, done, core_r, fa_r, fb_r, a1_r, b1_r, a2_r, b2_r, z_r, pw_r, qz_r, q_r, g_r,
    ga_r, gb_r, na_r, nb_r, ha_r, hb_r, ca_r, cb_r,
):
    x, c, z, y = (lax.axis_index(a) for a in AXES)
    other = 1 - c

    def at_x(o):
        return lax.rem(x + o, NX)

    def at_y(o):
        return lax.rem(y + o, NY)

    def at_z(o):
        return lax.rem(z + o, NZ)

    def xp(o):
        return {"x": at_x(o)}

    def yp(o):
        return {"y": at_y(o)}

    def zp(o):
        return {"z": at_z(o)}

    mate = {"c": other}
    plane = [
        (ox, oc, oy) for ox in (2, 1, 3, 0) for oy in (2, 1, 3, 0) for oc in (1, 0) if ox or oc or oy
    ]

    def in_plane(ox, oc, oy):
        return {"x": at_x(ox), "c": other if oc else c, "y": at_y(oy)}

    CORE, A1, B1, A2, B2, Z, PW, QZ, Q, G, GA, GB, CA, CB = range(14)

    def send(src, dst, kind, rs, to):
        pltpu.make_async_remote_copy(
            src_ref=src, dst_ref=dst, send_sem=done.at[kind], recv_sem=rs, device_id=to, device_id_type=MESH
        ).start()

    def handle(ref, sem):
        return pltpu.make_async_remote_copy(
            src_ref=ref, dst_ref=ref, send_sem=sem, recv_sem=sem, device_id=mate, device_id_type=MESH
        )

    def arrived(dst, rs):
        handle(dst, rs).wait_recv()

    barrier = pltpu.get_barrier_semaphore()
    for o in plane:
        pl.semaphore_signal(barrier, inc=1, device_id=in_plane(*o), device_id_type=MESH)
    for o in FAR_Z:
        pl.semaphore_signal(barrier, inc=1, device_id=zp(o), device_id_type=MESH)

    offs = (2, 1, 3, 0)
    blocks = [at_x(o) for o in offs]
    load_cot = [
        pltpu.make_async_copy(cot_hbm.at[:, pl.ds(i * FF, FF)], cot.at[i], ld.at[3 + i]) for i in range(2)
    ]
    load_tok = []
    for j in range(NX):
        for i, cc in enumerate((other, c)):
            start = pl.multiple_of(blocks[j] * 512 + cc * 256, 256)
            load_tok.append(
                pltpu.make_async_copy(tok_hbm.at[:, pl.ds(start, 256)], tok.at[2 * j + i], ld_t.at[2 * j + i])
            )
    load_pw = [
        pltpu.make_async_copy(h, pw.at[i, z], ld.at[i]) for i, h in enumerate((w_hbm, m_hbm, v_hbm))
    ]
    load_nxt = [
        pltpu.make_async_copy(nxt_hbm.at[:, pl.ds(k * 512, 512)], nxt.at[k], ld.at[5]) for k in range(NX)
    ]
    for cp in [load_cot[0], load_tok[0], load_cot[1], load_tok[1]]:
        cp.start()

    def rows_of(i):
        return jnp.transpose(tok[i])

    def block_grad(lhs, h):
        return jnp.dot(lhs, cot[h], preferred_element_type=f32).reshape(NZ, NY, ROWS, FF)

    def pass_on(src, o, to):
        slot = at_z(NZ - src)
        send(pw.at[:, slot], pw.at[:, slot], PW, pw_r.at[o - 1], zp(to))

    half = NZ // 2
    lower, upper = pl.ds(0, half), pl.ds(half, half)
    whole = pl.ds(0, NZ)
    via_next, via_prev = (2, 0), (1, 3)

    def gate_sum(j, k, zs=whole):
        yk = at_y(k)
        return own[j, 0, zs, yk] + take[j, 0, zs, yk].astype(f32)

    def up_sum(j, k, zs=whole):
        yk = at_y(k)
        return own[j, 1, zs, yk] + take[j, 1, zs, yk].astype(f32)

    def near_a(j, k, value):
        sa[j, k] = value.astype(bf16)
        send(sa.at[j, k], ra1.at[k, j - 1], A1, a1_r.at[k], xp(1 if j == 1 else 3))

    def near_b(j, i, zs, value):
        sb[j, 1 + i, zs] = value.astype(bf16)
        send(sb.at[j, 1 + i, zs], rb1.at[j, i, zs], B1, b1_r.at[j], yp((1, 3)[i]))

    def combine_gate(j):
        arrived(take.at[j, 0], core_r.at[j, 0])
        if j == 0:
            for k in (2, 1, 0, 3):
                sa[0, k] = gate_sum(0, k).astype(bf16)
                i, n = (0, via_next.index(k)) if k in via_next else (1, via_prev.index(k))
                send(sa.at[0, k], fa.at[i, n], A1, fa_r.at[i], xp(1 if i == 0 else 3))
        if j == 1:
            for k in via_prev:
                near_a(1, k, gate_sum(1, k))
        if j == 2:
            for k in via_next:
                near_a(2, k, gate_sum(2, k))

    def combine_up(j):
        arrived(take.at[j, 1], core_r.at[j, 1])
        sb[j, 0] = up_sum(j, 2).astype(bf16)
        for zs, o in ((lower, 1), (upper, 3)):
            send(sb.at[j, 0, zs], fb.at[j, zs], B1, fb_r.at[j], yp(o))
        near_b(j, 0, upper, up_sum(j, 1, upper))
        near_b(j, 1, lower, up_sum(j, 3, lower))

    def add_a(i):
        arrived(fa.at[i], fa_r.at[i])
        for n, k in enumerate((via_next, via_prev)[i]):
            near_a(1 + i, k, gate_sum(1 + i, k) + fa[i, n].astype(f32))

    def add_b(j):
        arrived(fb.at[j], fb_r.at[j])
        near_b(j, 0, lower, up_sum(j, 1, lower) + fb[j, lower].astype(f32))
        near_b(j, 1, upper, up_sum(j, 3, upper) + fb[j, upper].astype(f32))

    def second_a(k):
        total = gate_sum(NX - 1, k)
        arrived(ra1.at[k], a1_r.at[k])
        total += ra1[k, 0].astype(f32) + ra1[k, 1].astype(f32)
        if k:
            ta[k - 1] = total.astype(bf16)
            send(ta.at[k - 1], ra2.at[k - 1], A2, a2_r.at[0], yp(k))
        return total

    def second_b(j):
        total = up_sum(j, 0)
        arrived(rb1.at[j], b1_r.at[j])
        total += rb1[j, 0].astype(f32) + rb1[j, 1].astype(f32)
        o = offs[j]
        if o:
            tb[o - 1] = total.astype(bf16)
            send(tb.at[o - 1], rb2.at[o - 1], B2, b2_r.at[0], xp(o))
        return total

    def give_send(j, h):
        send(give.at[j, h], take.at[j, h], CORE, core_r.at[j, h], mate)

    for j in range(NX):
        if j:
            load_tok[2 * j].wait()
        else:
            load_cot[0].wait()
            load_tok[0].wait()
            for cp in load_tok[2:] + load_pw:
                cp.start()
        lhs = rows_of(2 * j)
        give[j, 0] = block_grad(lhs, 0).astype(bf16)
        if j == 0:
            pl.semaphore_wait(barrier, len(plane) + len(FAR_Z))
        give_send(j, 0)
        if j == 0:
            load_cot[1].wait()
        give[j, 1] = block_grad(lhs, 1).astype(bf16)
        give_send(j, 1)
        if j:
            combine_gate(j - 1)
            combine_up(j - 1)
        load_tok[2 * j + 1].wait()
        lhs = rows_of(2 * j + 1)
        own[j, 0] = block_grad(lhs, 0)
        own[j, 1] = block_grad(lhs, 1)
        if j == 0:
            for cp in load_pw:
                cp.wait()
            pass_on(0, 1, 1)
            pass_on(0, 7, 7)
            pass_on(0, 4, 4)
    combine_gate(NX - 1)
    combine_up(NX - 1)
    for cp in load_nxt:
        cp.start()
    add_a(0)
    add_b(0)
    add_a(1)
    add_b(1)
    add_b(2)
    add_b(3)
    arrived(pw.at[:, at_z(7)], pw_r.at[0])
    pass_on(1, 2, 1)
    arrived(pw.at[:, at_z(1)], pw_r.at[6])
    pass_on(7, 6, 7)
    second_b(0)
    second_a(2)
    second_a(1)
    second_b(1)
    second_b(2)
    second_a(3)
    total = second_a(0)
    arrived(pw.at[:, at_z(6)], pw_r.at[1])
    pass_on(2, 3, 1)
    arrived(pw.at[:, at_z(2)], pw_r.at[5])
    pass_on(6, 5, 7)
    arrived(ra2, a2_r.at[0])
    for k in range(NY - 1):
        total += ra2[k].astype(f32)
    tz[:, :, :FF] = total.astype(bf16)
    total = second_b(NX - 1)
    arrived(rb2, b2_r.at[0])
    for k in range(NX - 1):
        total += rb2[k].astype(f32)
    tz[:, :, FF:] = total.astype(bf16)

    for o in FAR_Z:
        send(tz.at[at_z(o)], rz.at[o - 1], Z, z_r.at[0], zp(o))
    grad = tz[z].astype(f32)
    arrived(rz, z_r.at[0])
    for o in range(NZ - 1):
        grad += rz[o].astype(f32)

    def fold(t):
        t = t * t
        t = jnp.sum(t, axis=0, keepdims=True)
        return t[:, 0:128] + t[:, 128:256] + t[:, 256:384] + t[:, 384:512]

    sqz[...] = jnp.concatenate([fold(grad[:, :FF]), fold(grad[:, FF:])], axis=0)
    for o in FAR_Z:
        send(sqz, rsqz.at[o - 1], QZ, qz_r.at[0], zp(o))
    gz[0] = grad.astype(bf16)
    both = sqz[...]
    arrived(rsqz, qz_r.at[0])
    for o in range(NZ - 1):
        both += rsqz[o]
    rsq[0] = both
    for i, o in enumerate(plane):
        send(rsq.at[0], rsq.at[1 + i], Q, q_r.at[0], in_plane(*o))
    for o in FAR_Z:
        send(gz.at[0], gz.at[o], G, g_r.at[0], zp(o))
    arrived(gz.at[pl.ds(1, NZ - 1)], g_r.at[0])
    for o in (3, 5, 4):
        arrived(pw.at[:, at_z(NZ - o)], pw_r.at[o - 1])
    arrived(rsq.at[pl.ds(1, len(plane))], q_r.at[0])
    both = jnp.sum(rsq[...], axis=0)
    limit = math.sqrt(D * FF)
    factor = jnp.minimum(1.0, limit / jnp.sqrt(jnp.sum(both, axis=1, keepdims=True) + 1e-06))
    gate_factor, up_factor = factor[0:1], factor[1:2]
    first_scale = 0.003 / (1.0 - 0.9**10)
    second_scale = 1.0 / (1.0 - 0.95**10)

    def moments(g, slot):
        clipped = jnp.concatenate([g[:, :FF] * gate_factor, g[:, FF:] * up_factor], axis=1)
        return 0.9 * pw[1, slot] + 0.1 * clipped, 0.95 * pw[2, slot] + 0.05 * clipped * clipped

    for o in range(NZ):
        k = at_z(NZ - o)
        first, second = moments(gz[o].astype(f32), k)
        low = pw[0, k] * (1.0 - 0.003 * 0.1) - (first * first_scale) / (jnp.sqrt(second * second_scale) + 1e-08)
        low = low.astype(bf16)
        wa[x, c, k, y] = low[:, :FF]
        wb[x, c, k, y] = low[:, FF:]

    def pa(ox, oy, lo=0, n=NZ):
        return wa.at[at_x(NX - ox), c, pl.ds(lo, n), at_y(NY - oy)]

    def pb(ox, oy, lo=0, n=NZ):
        return wb.at[at_x(NX - ox), c, pl.ds(lo, n), at_y(NY - oy)]

    def to_mate_a(ox, oy):
        send(pa(ox, oy), pa(ox, oy), CA, ca_r.at[ox], mate)

    def to_mate_b(ox, oy):
        send(pb(ox, oy), pb(ox, oy), CB, cb_r.at[ox], mate)

    def spread_a(oy):
        for i, o in enumerate((1, 3)):
            send(pa(0, oy), pa(0, oy), GA, na_r.at[i, oy], xp(o))
        to_mate_a(0, oy)

    def spread_b(ox):
        for i, o in enumerate((1, 3)):
            send(pb(ox, 0), pb(ox, 0), GB, nb_r.at[i, ox], yp(o))
        to_mate_b(ox, 0)

    for o in (1, 3, 2):
        send(pa(0, 0), pa(0, 0), GA, ga_r.at[o - 1], yp(o))
        send(pb(0, 0), pb(0, 0), GB, gb_r.at[o - 1], xp(o))
    spread_a(0)
    spread_b(0)

    first, second = moments(grad, z)
    nf_ref[...] = first
    nv_ref[...] = second

    def forward(o):
        arrived(pa(0, o), ga_r.at[o - 1])
        spread_a(o)
        arrived(pb(o, 0), gb_r.at[o - 1])
        spread_b(o)

    def relay(k):
        for i, o in enumerate((1, 3)):
            arrived(pa(o, k), na_r.at[i, k])
            part = pa(o, k, i * half, half)
            send(part, part, GA, ha_r.at[k], xp(o))
            to_mate_a(o, k)
            arrived(pb(k, o), nb_r.at[i, k])
            part = pb(k, o, i * half, half)
            send(part, part, GB, hb_r.at[k], yp(o))
            to_mate_b(k, o)

    def last(k):
        arrived(pa(2, k), ha_r.at[k])
        to_mate_a(2, k)
        arrived(pb(k, 2), hb_r.at[k])
        to_mate_b(k, 2)

    wa_k, wb_k = wa.reshape(NX, 512, FF), wb.reshape(NX, 512, FF)
    def mate_a(ox):
        arrived(wa.at[at_x(NX - ox), other], ca_r.at[ox])

    def mate_b(ox):
        arrived(wb.at[at_x(NX - ox), other], cb_r.at[ox])

    tile_rows = 512

    def multiply(acc, w_k, ox):
        k = at_x(NX - ox)

        def tile(i, _):
            r = pl.ds(pl.multiple_of(i * tile_rows, tile_rows), tile_rows)
            acc[r, :] = jnp.dot(nxt[k, r, :], w_k[k], preferred_element_type=f32)
            return 0

        lax.fori_loop(0, TOK // tile_rows, tile, 0)

    def finish():
        ks = [at_x(NX - ox) for ox in (1, 3, 2)]

        def tile(i, _):
            r = pl.ds(pl.multiple_of(i * tile_rows, tile_rows), tile_rows)
            gate, up = gate_acc[r, :], up_acc[r, :]
            for k in ks:
                gate += jnp.dot(nxt[k, r, :], wa_k[k], preferred_element_type=f32)
            for k in ks:
                up += jnp.dot(nxt[k, r, :], wb_k[k], preferred_element_type=f32)
            out_ref[r, :] = (gate / (1.0 + jnp.exp(-gate)) * up).astype(bf16)
            return 0

        lax.fori_loop(0, TOK // tile_rows, tile, 0)

    forward(1)
    forward(3)
    relay(0)
    forward(2)
    pltpu.make_async_copy(nxt, nxt, ld.at[5]).wait()
    relay(1)
    mate_a(0)
    multiply(gate_acc, wa_k, 0)
    relay(3)
    relay(2)
    last(0)
    last(1)
    last(3)
    mate_b(0)
    multiply(up_acc, wb_k, 0)
    last(2)
    for ox in (1, 3, 2):
        mate_a(ox)
        mate_b(ox)
    finish()
    rows64 = pl.ds(0, 15 * 64)
    bytes_of = {
        CORE: give, A1: sa, B1: sb, A2: ta, B2: tb, Z: tz.at[pl.ds(0, NZ - 1)], PW: pw.at[:, pl.ds(0, NZ - 1)],
        QZ: rsqz, Q: rsq.at[pl.ds(1, len(plane))], G: gz.at[pl.ds(1, NZ - 1)],
        GA: wa.reshape(D, FF).at[rows64], GB: wb.reshape(D, FF).at[rows64], CA: wa.at[:, c], CB: wb.at[:, c],
    }
    for kind, ref in bytes_of.items():
        handle(ref, done.at[kind]).wait_send()


def keep(a_ref, b_ref, c_ref, a_out, b_out, c_out, sem):
    moves = ((c_ref, c_out), (a_ref, a_out), (b_ref, b_out))
    copies = [pltpu.make_async_copy(s, d, sem.at[i]) for i, (s, d) in enumerate(moves)]
    for cp in copies:
        cp.start()
    for cp in copies:
        cp.wait()


def shards(tokens, grad_out, master_weight, first_moment, second_moment, next_tokens):
    any_ = pl.BlockSpec(memory_space=pltpu.HBM)
    V = pltpu.VMEM
    dma = pltpu.SemaphoreType.DMA

    block = (NX, 2, NZ, NY, ROWS, FF)
    piece = (NZ, ROWS, FF)
    scratch = [
        V((2 * NX, TOK, 256), bf16), V((2, TOK, FF), bf16), V((NX, TOK, 512), bf16), V((3, NZ, ROWS, 2 * FF), f32),
        V(block, f32), V(block, bf16), V(block, bf16),
        V((NX - 1, NY, *piece), bf16), V((NX, NY - 1, *piece), bf16), V((2, 2, *piece), bf16), V((NX, *piece), bf16),
        V((NY, 2, *piece), bf16), V((NX, 2, *piece), bf16),
        V((NY - 1, *piece), bf16), V((NX - 1, *piece), bf16), V((NY - 1, *piece), bf16), V((NX - 1, *piece), bf16),
        V((NZ, ROWS, 2 * FF), bf16), V((NZ - 1, ROWS, 2 * FF), bf16),
        V((2, 128), f32), V((NZ - 1, 2, 128), f32), V((NX * NC * NY, 2, 128), f32),
        V((NZ, ROWS, 2 * FF), bf16),
        V((NX, NC, NZ, NY, ROWS, FF), bf16), V((NX, NC, NZ, NY, ROWS, FF), bf16),
        V((TOK, FF), f32), V((TOK, FF), f32),
        dma((2 * NX,)), dma((6,)), dma((14,)),
        dma((NX, 2)), dma((2,)), dma((NX,)), dma((NY,)), dma((NX,)), dma((1,)), dma((1,)), dma((1,)),
        dma((NZ - 1,)), dma((1,)), dma((1,)), dma((1,)),
        dma((NY - 1,)), dma((NX - 1,)), dma((2, NY)), dma((2, NX)), dma((NY,)), dma((NX,)), dma((NX,)), dma((NX,)),
    ]
    shapes = (
        jax.ShapeDtypeStruct((ROWS, 2 * FF), f32),
        jax.ShapeDtypeStruct((ROWS, 2 * FF), f32),
        jax.ShapeDtypeStruct((TOK, FF), bf16),
    )
    inputs = (tokens, grad_out, master_weight, first_moment, second_moment, next_tokens)
    results = pl.pallas_call(
        body,
        out_shape=shapes,
        in_specs=[any_] * 6,
        out_specs=(pl.BlockSpec(memory_space=pltpu.VMEM),) * 3,
        scratch_shapes=scratch,
        compiler_params=pltpu.CompilerParams(
            collective_id=0, has_side_effects=True, vmem_limit_bytes=103 * 512 * 1024
        ),
    )(*(pltpu.with_memory_space_constraint(a, pltpu.HBM) for a in inputs))
    return pl.pallas_call(
        keep,
        out_shape=shapes,
        in_specs=[any_] * 3,
        out_specs=(any_,) * 3,
        scratch_shapes=[dma((3,))],
        compiler_params=pltpu.CompilerParams(vmem_limit_bytes=2 * 1024 * 1024),
    )(*results)


def solution(mesh):
    split = Mesh(mesh.devices.reshape(NX, NC, NZ, NY), AXES)
    rows = P(AXES, None)
    return jax.shard_map(
        shards, mesh=split, in_specs=(rows,) * 6, out_specs=(rows,) * 3, check_vma=False
    )
```

```python
import math

import jax
import jax.numpy as jnp
from jax import lax
from jax.experimental import pallas as pl
from jax.experimental.pallas import tpu as pltpu
from jax.sharding import Mesh
from jax.sharding import PartitionSpec as P

NX, NC, NZ, NY = 4, 2, 8, 4
ROWS = 8
D = 2048
FF = 512
TOK = 1024
AXES = ("x", "c", "z", "y")
MESH = pl.DeviceIdType.MESH
FAR_Z = (4, 3, 5, 2, 6, 1, 7)
f32 = jnp.float32
bf16 = jnp.bfloat16


def body(
    tok_hbm, cot_hbm, w_hbm, m_hbm, v_hbm, nxt_hbm,
    nf_ref, nv_ref, out_ref,
    tok, cot, nxt, pw, own, give, take,
    sa, sb, fa, fb, ra1, rb1, ta, tb, ra2, rb2, tz, rz, sqz, rsqz, rsq, gz, wa, wb, gate_acc, up_acc,
    ld_t, ld, done, core_r, fa_r, fb_r, a1_r, b1_r, a2_r, b2_r, z_r, pw_r, qz_r, q_r, g_r,
    ga_r, gb_r, na_r, nb_r, ha_r, hb_r, ca_r, cb_r,
):
    x, c, z, y = (lax.axis_index(a) for a in AXES)
    other = 1 - c

    def at_x(o):
        return lax.rem(x + o, NX)

    def at_y(o):
        return lax.rem(y + o, NY)

    def at_z(o):
        return lax.rem(z + o, NZ)

    def xp(o):
        return {"x": at_x(o)}

    def yp(o):
        return {"y": at_y(o)}

    def zp(o):
        return {"z": at_z(o)}

    mate = {"c": other}
    plane = [
        (ox, oc, oy) for ox in (2, 1, 3, 0) for oy in (2, 1, 3, 0) for oc in (1, 0) if ox or oc or oy
    ]

    def in_plane(ox, oc, oy):
        return {"x": at_x(ox), "c": other if oc else c, "y": at_y(oy)}

    CORE, A1, B1, A2, B2, Z, PW, QZ, Q, G, GA, GB, CA, CB = range(14)

    def send(src, dst, kind, rs, to):
        pltpu.make_async_remote_copy(
            src_ref=src, dst_ref=dst, send_sem=done.at[kind], recv_sem=rs, device_id=to, device_id_type=MESH
        ).start()

    def handle(ref, sem):
        return pltpu.make_async_remote_copy(
            src_ref=ref, dst_ref=ref, send_sem=sem, recv_sem=sem, device_id=mate, device_id_type=MESH
        )

    def arrived(dst, rs):
        handle(dst, rs).wait_recv()

    barrier = pltpu.get_barrier_semaphore()
    for o in plane:
        pl.semaphore_signal(barrier, inc=1, device_id=in_plane(*o), device_id_type=MESH)
    for o in FAR_Z:
        pl.semaphore_signal(barrier, inc=1, device_id=zp(o), device_id_type=MESH)

    offs = (2, 1, 3, 0)
    blocks = [at_x(o) for o in offs]
    load_cot = [
        pltpu.make_async_copy(cot_hbm.at[:, pl.ds(i * FF, FF)], cot.at[i], ld.at[3 + i]) for i in range(2)
    ]
    load_tok = []
    for j in range(NX):
        for i, cc in enumerate((other, c)):
            start = pl.multiple_of(blocks[j] * 512 + cc * 256, 256)
            load_tok.append(
                pltpu.make_async_copy(tok_hbm.at[:, pl.ds(start, 256)], tok.at[2 * j + i], ld_t.at[2 * j + i])
            )
    load_pw = [
        pltpu.make_async_copy(h, pw.at[i, z], ld.at[i]) for i, h in enumerate((w_hbm, m_hbm, v_hbm))
    ]
    load_nxt = [
        pltpu.make_async_copy(nxt_hbm.at[:, pl.ds(k * 512, 512)], nxt.at[k], ld.at[5]) for k in range(NX)
    ]
    for cp in [load_cot[0], load_tok[0], load_cot[1], load_tok[1]]:
        cp.start()

    def rows_of(i):
        return jnp.transpose(tok[i])

    def block_grad(lhs, h):
        return jnp.dot(lhs, cot[h], preferred_element_type=f32).reshape(NZ, NY, ROWS, FF)

    def pass_on(src, o, to):
        slot = at_z(NZ - src)
        send(pw.at[:, slot], pw.at[:, slot], PW, pw_r.at[o - 1], zp(to))

    half = NZ // 2
    lower, upper = pl.ds(0, half), pl.ds(half, half)
    whole = pl.ds(0, NZ)
    via_next, via_prev = (2, 0), (1, 3)

    def gate_sum(j, k, zs=whole):
        yk = at_y(k)
        return own[j, 0, zs, yk] + take[j, 0, zs, yk].astype(f32)

    def up_sum(j, k, zs=whole):
        yk = at_y(k)
        return own[j, 1, zs, yk] + take[j, 1, zs, yk].astype(f32)

    def near_a(j, k, value):
        sa[j, k] = value.astype(bf16)
        send(sa.at[j, k], ra1.at[k, j - 1], A1, a1_r.at[k], xp(1 if j == 1 else 3))

    def near_b(j, i, zs, value):
        sb[j, 1 + i, zs] = value.astype(bf16)
        send(sb.at[j, 1 + i, zs], rb1.at[j, i, zs], B1, b1_r.at[j], yp((1, 3)[i]))

    def combine_gate(j):
        arrived(take.at[j, 0], core_r.at[j, 0])
        if j == 0:
            for k in (2, 1, 0, 3):
                sa[0, k] = gate_sum(0, k).astype(bf16)
                i, n = (0, via_next.index(k)) if k in via_next else (1, via_prev.index(k))
                send(sa.at[0, k], fa.at[i, n], A1, fa_r.at[i], xp(1 if i == 0 else 3))
        if j == 1:
            for k in via_prev:
                near_a(1, k, gate_sum(1, k))
        if j == 2:
            for k in via_next:
                near_a(2, k, gate_sum(2, k))

    def combine_up(j):
        arrived(take.at[j, 1], core_r.at[j, 1])
        sb[j, 0] = up_sum(j, 2).astype(bf16)
        for zs, o in ((lower, 1), (upper, 3)):
            send(sb.at[j, 0, zs], fb.at[j, zs], B1, fb_r.at[j], yp(o))
        near_b(j, 0, upper, up_sum(j, 1, upper))
        near_b(j, 1, lower, up_sum(j, 3, lower))

    def add_a(i):
        arrived(fa.at[i], fa_r.at[i])
        for n, k in enumerate((via_next, via_prev)[i]):
            near_a(1 + i, k, gate_sum(1 + i, k) + fa[i, n].astype(f32))

    def add_b(j):
        arrived(fb.at[j], fb_r.at[j])
        near_b(j, 0, lower, up_sum(j, 1, lower) + fb[j, lower].astype(f32))
        near_b(j, 1, upper, up_sum(j, 3, upper) + fb[j, upper].astype(f32))

    def second_a(k):
        total = gate_sum(NX - 1, k)
        arrived(ra1.at[k], a1_r.at[k])
        total += ra1[k, 0].astype(f32) + ra1[k, 1].astype(f32)
        if k:
            ta[k - 1] = total.astype(bf16)
            send(ta.at[k - 1], ra2.at[k - 1], A2, a2_r.at[0], yp(k))
        return total

    def second_b(j):
        total = up_sum(j, 0)
        arrived(rb1.at[j], b1_r.at[j])
        total += rb1[j, 0].astype(f32) + rb1[j, 1].astype(f32)
        o = offs[j]
        if o:
            tb[o - 1] = total.astype(bf16)
            send(tb.at[o - 1], rb2.at[o - 1], B2, b2_r.at[0], xp(o))
        return total

    def give_send(j, h):
        send(give.at[j, h], take.at[j, h], CORE, core_r.at[j, h], mate)

    for j in range(NX):
        if j:
            load_tok[2 * j].wait()
        else:
            load_cot[0].wait()
            load_tok[0].wait()
            for cp in load_tok[2:] + load_pw:
                cp.start()
        lhs = rows_of(2 * j)
        give[j, 0] = block_grad(lhs, 0).astype(bf16)
        if j == 0:
            pl.semaphore_wait(barrier, len(plane) + len(FAR_Z))
        give_send(j, 0)
        if j == 0:
            load_cot[1].wait()
        give[j, 1] = block_grad(lhs, 1).astype(bf16)
        give_send(j, 1)
        if j:
            combine_gate(j - 1)
            combine_up(j - 1)
        load_tok[2 * j + 1].wait()
        lhs = rows_of(2 * j + 1)
        own[j, 0] = block_grad(lhs, 0)
        own[j, 1] = block_grad(lhs, 1)
        if j == 0:
            for cp in load_pw:
                cp.wait()
            pass_on(0, 1, 1)
            pass_on(0, 7, 7)
            pass_on(0, 4, 4)
    combine_gate(NX - 1)
    combine_up(NX - 1)
    for cp in load_nxt:
        cp.start()
    add_a(0)
    add_b(0)
    add_a(1)
    add_b(1)
    add_b(2)
    add_b(3)
    arrived(pw.at[:, at_z(7)], pw_r.at[0])
    pass_on(1, 2, 1)
    arrived(pw.at[:, at_z(1)], pw_r.at[6])
    pass_on(7, 6, 7)
    second_b(0)
    second_a(2)
    second_a(1)
    second_b(1)
    second_b(2)
    second_a(3)
    total = second_a(0)
    arrived(pw.at[:, at_z(6)], pw_r.at[1])
    pass_on(2, 3, 1)
    arrived(pw.at[:, at_z(2)], pw_r.at[5])
    pass_on(6, 5, 7)
    arrived(ra2, a2_r.at[0])
    for k in range(NY - 1):
        total += ra2[k].astype(f32)
    tz[:, :, :FF] = total.astype(bf16)
    total = second_b(NX - 1)
    arrived(rb2, b2_r.at[0])
    for k in range(NX - 1):
        total += rb2[k].astype(f32)
    tz[:, :, FF:] = total.astype(bf16)

    for o in FAR_Z:
        send(tz.at[at_z(o)], rz.at[o - 1], Z, z_r.at[0], zp(o))
    grad = tz[z].astype(f32)
    arrived(rz, z_r.at[0])
    for o in range(NZ - 1):
        grad += rz[o].astype(f32)

    def fold(t):
        t = t * t
        t = jnp.sum(t, axis=0, keepdims=True)
        return t[:, 0:128] + t[:, 128:256] + t[:, 256:384] + t[:, 384:512]

    sqz[...] = jnp.concatenate([fold(grad[:, :FF]), fold(grad[:, FF:])], axis=0)
    for o in FAR_Z:
        send(sqz, rsqz.at[o - 1], QZ, qz_r.at[0], zp(o))
    gz[0] = grad.astype(bf16)
    both = sqz[...]
    arrived(rsqz, qz_r.at[0])
    for o in range(NZ - 1):
        both += rsqz[o]
    rsq[0] = both
    for i, o in enumerate(plane):
        send(rsq.at[0], rsq.at[1 + i], Q, q_r.at[0], in_plane(*o))
    for o in FAR_Z:
        send(gz.at[0], gz.at[o], G, g_r.at[0], zp(o))
    arrived(gz.at[pl.ds(1, NZ - 1)], g_r.at[0])
    for o in (3, 5, 4):
        arrived(pw.at[:, at_z(NZ - o)], pw_r.at[o - 1])
    arrived(rsq.at[pl.ds(1, len(plane))], q_r.at[0])
    both = jnp.sum(rsq[...], axis=0)
    limit = math.sqrt(D * FF)
    factor = jnp.minimum(1.0, limit / jnp.sqrt(jnp.sum(both, axis=1, keepdims=True) + 1e-06))
    gate_factor, up_factor = factor[0:1], factor[1:2]
    first_scale = 0.003 / (1.0 - 0.9**10)
    second_scale = 1.0 / (1.0 - 0.95**10)

    def moments(g, slot):
        clipped = jnp.concatenate([g[:, :FF] * gate_factor, g[:, FF:] * up_factor], axis=1)
        return 0.9 * pw[1, slot] + 0.1 * clipped, 0.95 * pw[2, slot] + 0.05 * clipped * clipped

    for o in range(NZ):
        k = at_z(NZ - o)
        first, second = moments(gz[o].astype(f32), k)
        low = pw[0, k] * (1.0 - 0.003 * 0.1) - (first * first_scale) / (jnp.sqrt(second * second_scale) + 1e-08)
        low = low.astype(bf16)
        wa[x, c, k, y] = low[:, :FF]
        wb[x, c, k, y] = low[:, FF:]

    def pa(ox, oy, lo=0, n=NZ):
        return wa.at[at_x(NX - ox), c, pl.ds(lo, n), at_y(NY - oy)]

    def pb(ox, oy, lo=0, n=NZ):
        return wb.at[at_x(NX - ox), c, pl.ds(lo, n), at_y(NY - oy)]

    def to_mate_a(ox, oy):
        send(pa(ox, oy), pa(ox, oy), CA, ca_r.at[ox], mate)

    def to_mate_b(ox, oy):
        send(pb(ox, oy), pb(ox, oy), CB, cb_r.at[ox], mate)

    def spread_a(oy):
        for i, o in enumerate((1, 3)):
            send(pa(0, oy), pa(0, oy), GA, na_r.at[i, oy], xp(o))
        to_mate_a(0, oy)

    def spread_b(ox):
        for i, o in enumerate((1, 3)):
            send(pb(ox, 0), pb(ox, 0), GB, nb_r.at[i, ox], yp(o))
        to_mate_b(ox, 0)

    for o in (1, 3, 2):
        send(pa(0, 0), pa(0, 0), GA, ga_r.at[o - 1], yp(o))
        send(pb(0, 0), pb(0, 0), GB, gb_r.at[o - 1], xp(o))
    spread_a(0)
    spread_b(0)

    first, second = moments(grad, z)
    nf_ref[...] = first
    nv_ref[...] = second

    def forward(o):
        arrived(pa(0, o), ga_r.at[o - 1])
        spread_a(o)
        arrived(pb(o, 0), gb_r.at[o - 1])
        spread_b(o)

    def relay(k):
        for i, o in enumerate((1, 3)):
            arrived(pa(o, k), na_r.at[i, k])
            part = pa(o, k, i * half, half)
            send(part, part, GA, ha_r.at[k], xp(o))
            to_mate_a(o, k)
            arrived(pb(k, o), nb_r.at[i, k])
            part = pb(k, o, i * half, half)
            send(part, part, GB, hb_r.at[k], yp(o))
            to_mate_b(k, o)

    def last(k):
        arrived(pa(2, k), ha_r.at[k])
        to_mate_a(2, k)
        arrived(pb(k, 2), hb_r.at[k])
        to_mate_b(k, 2)

    wa_k, wb_k = wa.reshape(NX, 512, FF), wb.reshape(NX, 512, FF)
    def mate_a(ox):
        arrived(wa.at[at_x(NX - ox), other], ca_r.at[ox])

    def mate_b(ox):
        arrived(wb.at[at_x(NX - ox), other], cb_r.at[ox])

    tile_rows = 512

    tile_rows = 512

    def multiply(acc, w_k, *oxs):
        ks = [at_x(NX - ox) for ox in oxs]

        def tile(i, _):
            r = pl.ds(pl.multiple_of(i * tile_rows, tile_rows), tile_rows)
            terms = [jnp.dot(nxt[k, r, :], w_k[k], preferred_element_type=f32) for k in ks]
            acc[r, :] = sum(terms[1:], terms[0]) if 0 in oxs else sum(terms, acc[r, :])
            return 0

        lax.fori_loop(0, TOK // tile_rows, tile, 0)

    def finish():
        k = at_x(NX - 2)

        def tile(i, _):
            r = pl.ds(pl.multiple_of(i * tile_rows, tile_rows), tile_rows)
            gate = gate_acc[r, :] + jnp.dot(nxt[k, r, :], wa_k[k], preferred_element_type=f32)
            up = up_acc[r, :] + jnp.dot(nxt[k, r, :], wb_k[k], preferred_element_type=f32)
            out_ref[r, :] = (gate / (1.0 + jnp.exp(-gate)) * up).astype(bf16)
            return 0

        lax.fori_loop(0, TOK // tile_rows, tile, 0)

    forward(1)
    forward(3)
    relay(0)
    forward(2)
    pltpu.make_async_copy(nxt, nxt, ld.at[5]).wait()
    relay(1)
    mate_a(0)
    multiply(gate_acc, wa_k, 0)
    relay(3)
    relay(2)
    last(0)
    last(1)
    mate_b(0)
    multiply(up_acc, wb_k, 0)
    last(3)
    mate_a(1)
    mate_a(3)
    multiply(gate_acc, wa_k, 1, 3)
    last(2)
    mate_b(1)
    mate_b(3)
    multiply(up_acc, wb_k, 1, 3)
    mate_a(2)
    mate_b(2)
    finish()
    rows64 = pl.ds(0, 15 * 64)
    bytes_of = {
        CORE: give, A1: sa, B1: sb, A2: ta, B2: tb, Z: tz.at[pl.ds(0, NZ - 1)], PW: pw.at[:, pl.ds(0, NZ - 1)],
        QZ: rsqz, Q: rsq.at[pl.ds(1, len(plane))], G: gz.at[pl.ds(1, NZ - 1)],
        GA: wa.reshape(D, FF).at[rows64], GB: wb.reshape(D, FF).at[rows64], CA: wa.at[:, c], CB: wb.at[:, c],
    }
    for kind, ref in bytes_of.items():
        handle(ref, done.at[kind]).wait_send()


def keep(a_ref, b_ref, c_ref, a_out, b_out, c_out, sem):
    moves = ((c_ref, c_out), (a_ref, a_out), (b_ref, b_out))
    copies = [pltpu.make_async_copy(s, d, sem.at[i]) for i, (s, d) in enumerate(moves)]
    for cp in copies:
        cp.start()
    for cp in copies:
        cp.wait()


def shards(tokens, grad_out, master_weight, first_moment, second_moment, next_tokens):
    any_ = pl.BlockSpec(memory_space=pltpu.HBM)
    V = pltpu.VMEM
    dma = pltpu.SemaphoreType.DMA

    block = (NX, 2, NZ, NY, ROWS, FF)
    piece = (NZ, ROWS, FF)
    scratch = [
        V((2 * NX, TOK, 256), bf16), V((2, TOK, FF), bf16), V((NX, TOK, 512), bf16), V((3, NZ, ROWS, 2 * FF), f32),
        V(block, f32), V(block, bf16), V(block, bf16),
        V((NX - 1, NY, *piece), bf16), V((NX, NY - 1, *piece), bf16), V((2, 2, *piece), bf16), V((NX, *piece), bf16),
        V((NY, 2, *piece), bf16), V((NX, 2, *piece), bf16),
        V((NY - 1, *piece), bf16), V((NX - 1, *piece), bf16), V((NY - 1, *piece), bf16), V((NX - 1, *piece), bf16),
        V((NZ, ROWS, 2 * FF), bf16), V((NZ - 1, ROWS, 2 * FF), bf16),
        V((2, 128), f32), V((NZ - 1, 2, 128), f32), V((NX * NC * NY, 2, 128), f32),
        V((NZ, ROWS, 2 * FF), bf16),
        V((NX, NC, NZ, NY, ROWS, FF), bf16), V((NX, NC, NZ, NY, ROWS, FF), bf16),
        V((TOK, FF), f32), V((TOK, FF), f32),
        dma((2 * NX,)), dma((6,)), dma((14,)),
        dma((NX, 2)), dma((2,)), dma((NX,)), dma((NY,)), dma((NX,)), dma((1,)), dma((1,)), dma((1,)),
        dma((NZ - 1,)), dma((1,)), dma((1,)), dma((1,)),
        dma((NY - 1,)), dma((NX - 1,)), dma((2, NY)), dma((2, NX)), dma((NY,)), dma((NX,)), dma((NX,)), dma((NX,)),
    ]
    shapes = (
        jax.ShapeDtypeStruct((ROWS, 2 * FF), f32),
        jax.ShapeDtypeStruct((ROWS, 2 * FF), f32),
        jax.ShapeDtypeStruct((TOK, FF), bf16),
    )
    inputs = (tokens, grad_out, master_weight, first_moment, second_moment, next_tokens)
    results = pl.pallas_call(
        body,
        out_shape=shapes,
        in_specs=[any_] * 6,
        out_specs=(pl.BlockSpec(memory_space=pltpu.VMEM),) * 3,
        scratch_shapes=scratch,
        compiler_params=pltpu.CompilerParams(
            collective_id=0, has_side_effects=True, vmem_limit_bytes=103 * 512 * 1024
        ),
    )(*(pltpu.with_memory_space_constraint(a, pltpu.HBM) for a in inputs))
    return pl.pallas_call(
        keep,
        out_shape=shapes,
        in_specs=[any_] * 3,
        out_specs=(any_,) * 3,
        scratch_shapes=[dma((3,))],
        compiler_params=pltpu.CompilerParams(vmem_limit_bytes=2 * 1024 * 1024),
    )(*results)


def solution(mesh):
    split = Mesh(mesh.devices.reshape(NX, NC, NZ, NY), AXES)
    rows = P(AXES, None)
    return jax.shard_map(
        shards, mesh=split, in_specs=(rows,) * 6, out_specs=(rows,) * 3, check_vma=False
    )
```

```python
import math

import jax
import jax.numpy as jnp
from jax import lax
from jax.experimental import pallas as pl
from jax.experimental.pallas import tpu as pltpu
from jax.sharding import Mesh
from jax.sharding import PartitionSpec as P

NX, NC, NZ, NY = 4, 2, 8, 4
ROWS = 8
D = 2048
FF = 512
TOK = 1024
AXES = ("x", "c", "z", "y")
MESH = pl.DeviceIdType.MESH
FAR_Z = (4, 3, 5, 2, 6, 1, 7)
f32 = jnp.float32
bf16 = jnp.bfloat16


def body(
    tok_hbm, cot_hbm, w_hbm, m_hbm, v_hbm, nxt_hbm,
    nf_ref, nv_ref, out_ref,
    tok, cot, nxt, pw, own, give, take,
    sa, sb, fa, fb, ra1, rb1, ta, tb, ra2, rb2, tz, rz, sqz, rsqz, rsq, gz, wa, wb, gate_acc, up_acc,
    ld_t, ld, done, core_r, fa_r, fb_r, a1_r, b1_r, a2_r, b2_r, z_r, pw_r, qz_r, q_r, g_r,
    ga_r, gb_r, na_r, nb_r, ha_r, hb_r, ca_r, cb_r,
):
    x, c, z, y = (lax.axis_index(a) for a in AXES)
    other = 1 - c

    def at_x(o):
        return lax.rem(x + o, NX)

    def at_y(o):
        return lax.rem(y + o, NY)

    def at_z(o):
        return lax.rem(z + o, NZ)

    def xp(o):
        return {"x": at_x(o)}

    def yp(o):
        return {"y": at_y(o)}

    def zp(o):
        return {"z": at_z(o)}

    mate = {"c": other}
    plane = [
        (ox, oc, oy) for ox in (2, 1, 3, 0) for oy in (2, 1, 3, 0) for oc in (1, 0) if ox or oc or oy
    ]

    def in_plane(ox, oc, oy):
        return {"x": at_x(ox), "c": other if oc else c, "y": at_y(oy)}

    CORE = A1 = B1 = A2 = B2 = 0
    Z = PW = G = GA = GB = CA = 1
    CB, QZ, Q = 2, 3, 4

    def send(src, dst, kind, rs, to):
        pltpu.make_async_remote_copy(
            src_ref=src, dst_ref=dst, send_sem=done.at[kind], recv_sem=rs, device_id=to, device_id_type=MESH
        ).start()

    def handle(ref, sem):
        return pltpu.make_async_remote_copy(
            src_ref=ref, dst_ref=ref, send_sem=sem, recv_sem=sem, device_id=mate, device_id_type=MESH
        )

    def arrived(dst, rs):
        handle(dst, rs).wait_recv()

    barrier = pltpu.get_barrier_semaphore()
    for o in plane:
        pl.semaphore_signal(barrier, inc=1, device_id=in_plane(*o), device_id_type=MESH)
    for o in FAR_Z:
        pl.semaphore_signal(barrier, inc=1, device_id=zp(o), device_id_type=MESH)

    offs = (2, 1, 3, 0)
    blocks = [at_x(o) for o in offs]
    load_cot = [
        pltpu.make_async_copy(cot_hbm.at[:, pl.ds(i * FF, FF)], cot.at[i], ld.at[3 + i]) for i in range(2)
    ]
    load_tok = []
    for j in range(NX):
        for i, cc in enumerate((other, c)):
            start = pl.multiple_of(blocks[j] * 512 + cc * 256, 256)
            load_tok.append(
                pltpu.make_async_copy(tok_hbm.at[:, pl.ds(start, 256)], tok.at[2 * j + i], ld_t.at[2 * j + i])
            )
    load_pw = [
        pltpu.make_async_copy(h, pw.at[i, z], ld.at[i]) for i, h in enumerate((w_hbm, m_hbm, v_hbm))
    ]
    load_nxt = [
        pltpu.make_async_copy(nxt_hbm.at[:, pl.ds(k * 512, 512)], nxt.at[k], ld.at[5]) for k in range(NX)
    ]
    for cp in [load_cot[0], load_tok[0], load_cot[1], load_tok[1]]:
        cp.start()

    def rows_of(i):
        return jnp.transpose(tok[i])

    def block_grad(lhs, h):
        return jnp.dot(lhs, cot[h], preferred_element_type=f32).reshape(NZ, NY, ROWS, FF)

    def pass_on(src, o, to):
        slot = at_z(NZ - src)
        send(pw.at[:, slot], pw.at[:, slot], PW, pw_r.at[o - 1], zp(to))

    half = NZ // 2
    lower, upper = pl.ds(0, half), pl.ds(half, half)
    whole = pl.ds(0, NZ)
    via_next, via_prev = (2, 0), (1, 3)

    def gate_sum(j, k, zs=whole):
        yk = at_y(k)
        return own[j, 0, zs, yk] + take[j, 0, zs, yk].astype(f32)

    def up_sum(j, k, zs=whole):
        yk = at_y(k)
        return own[j, 1, zs, yk] + take[j, 1, zs, yk].astype(f32)

    def near_a(j, k, value):
        sa[j, k] = value.astype(bf16)
        send(sa.at[j, k], ra1.at[k, j - 1], A1, a1_r.at[k], xp(1 if j == 1 else 3))

    def near_b(j, i, zs, value):
        sb[j, 1 + i, zs] = value.astype(bf16)
        send(sb.at[j, 1 + i, zs], rb1.at[j, i, zs], B1, b1_r.at[j], yp((1, 3)[i]))

    def combine_gate(j):
        arrived(take.at[j, 0], core_r.at[j, 0])
        if j == 0:
            for k in (2, 1, 0, 3):
                sa[0, k] = gate_sum(0, k).astype(bf16)
                i, n = (0, via_next.index(k)) if k in via_next else (1, via_prev.index(k))
                send(sa.at[0, k], fa.at[i, n], A1, fa_r.at[i], xp(1 if i == 0 else 3))
        if j == 1:
            for k in via_prev:
                near_a(1, k, gate_sum(1, k))
        if j == 2:
            near_a(2, 2, gate_sum(2, 2))

    def combine_up(j):
        arrived(take.at[j, 1], core_r.at[j, 1])
        sb[j, 0] = up_sum(j, 2).astype(bf16)
        for zs, o in ((lower, 1), (upper, 3)):
            send(sb.at[j, 0, zs], fb.at[j, zs], B1, fb_r.at[j], yp(o))
        near_b(j, 0, upper, up_sum(j, 1, upper))
        near_b(j, 1, lower, up_sum(j, 3, lower))

    def add_a(i):
        arrived(fa.at[i], fa_r.at[i])
        for n, k in enumerate((via_next, via_prev)[i]):
            near_a(1 + i, k, gate_sum(1 + i, k) + fa[i, n].astype(f32))

    def add_b(j):
        arrived(fb.at[j], fb_r.at[j])
        near_b(j, 0, lower, up_sum(j, 1, lower) + fb[j, lower].astype(f32))
        near_b(j, 1, upper, up_sum(j, 3, upper) + fb[j, upper].astype(f32))

    def second_a(k):
        total = gate_sum(NX - 1, k)
        arrived(ra1.at[k], a1_r.at[k])
        total += ra1[k, 0].astype(f32) + ra1[k, 1].astype(f32)
        if k:
            ta[k - 1] = total.astype(bf16)
            send(ta.at[k - 1], ra2.at[k - 1], A2, a2_r.at[0], yp(k))
        return total

    def second_b(j):
        total = up_sum(j, 0)
        arrived(rb1.at[j], b1_r.at[j])
        total += rb1[j, 0].astype(f32) + rb1[j, 1].astype(f32)
        o = offs[j]
        if o:
            tb[o - 1] = total.astype(bf16)
            send(tb.at[o - 1], rb2.at[o - 1], B2, b2_r.at[0], xp(o))
        return total

    def give_send(j, h):
        send(give.at[j, h], take.at[j, h], CORE, core_r.at[j, h], mate)

    for j in range(NX):
        if j:
            load_tok[2 * j].wait()
        else:
            load_cot[0].wait()
            load_tok[0].wait()
            for cp in load_tok[2:] + load_pw:
                cp.start()
        lhs = rows_of(2 * j)
        give[j, 0] = block_grad(lhs, 0).astype(bf16)
        if j == 0:
            pl.semaphore_wait(barrier, len(plane) + len(FAR_Z))
        give_send(j, 0)
        if j == 0:
            load_cot[1].wait()
        give[j, 1] = block_grad(lhs, 1).astype(bf16)
        give_send(j, 1)
        if j:
            combine_gate(j - 1)
            combine_up(j - 1)
        if j == NX - 1:
            add_b(0)
        load_tok[2 * j + 1].wait()
        lhs = rows_of(2 * j + 1)
        own[j, 0] = block_grad(lhs, 0)
        own[j, 1] = block_grad(lhs, 1)
        if j == 0:
            for cp in load_pw:
                cp.wait()
            pass_on(0, 1, 1)
            pass_on(0, 7, 7)
            pass_on(0, 4, 4)
    combine_gate(NX - 1)
    add_b(1)
    add_a(0)
    add_a(1)
    near_a(2, 0, gate_sum(2, 0))
    add_b(2)
    combine_up(NX - 1)
    for cp in load_nxt:
        cp.start()
    arrived(pw.at[:, at_z(7)], pw_r.at[0])
    pass_on(1, 2, 1)
    arrived(pw.at[:, at_z(1)], pw_r.at[6])
    pass_on(7, 6, 7)
    second_b(0)
    second_a(2)
    add_b(3)
    second_b(1)
    second_a(1)
    second_b(2)
    second_a(3)
    total = second_a(0)
    arrived(pw.at[:, at_z(6)], pw_r.at[1])
    pass_on(2, 3, 1)
    arrived(pw.at[:, at_z(2)], pw_r.at[5])
    pass_on(6, 5, 7)
    arrived(ra2, a2_r.at[0])
    for k in range(NY - 1):
        total += ra2[k].astype(f32)
    tz[:, :, :FF] = total.astype(bf16)
    total = second_b(NX - 1)
    arrived(rb2, b2_r.at[0])
    for k in range(NX - 1):
        total += rb2[k].astype(f32)
    tz[:, :, FF:] = total.astype(bf16)

    for o in FAR_Z:
        send(tz.at[at_z(o)], rz.at[o - 1], Z, z_r.at[0], zp(o))
    grad = tz[z].astype(f32)
    arrived(rz, z_r.at[0])
    for o in range(NZ - 1):
        grad += rz[o].astype(f32)

    def fold(t):
        t = t * t
        t = jnp.sum(t, axis=0, keepdims=True)
        return t[:, 0:128] + t[:, 128:256] + t[:, 256:384] + t[:, 384:512]

    sqz[...] = jnp.concatenate([fold(grad[:, :FF]), fold(grad[:, FF:])], axis=0)
    for o in FAR_Z:
        send(sqz, rsqz.at[o - 1], QZ, qz_r.at[0], zp(o))
    gz[0] = grad.astype(bf16)
    both = sqz[...]
    arrived(rsqz, qz_r.at[0])
    for o in range(NZ - 1):
        both += rsqz[o]
    rsq[0] = both
    for i, o in enumerate(plane):
        send(rsq.at[0], rsq.at[1 + i], Q, q_r.at[0], in_plane(*o))
    for o in FAR_Z:
        send(gz.at[0], gz.at[o], G, g_r.at[0], zp(o))
    arrived(gz.at[pl.ds(1, NZ - 1)], g_r.at[0])
    for o in (3, 5, 4):
        arrived(pw.at[:, at_z(NZ - o)], pw_r.at[o - 1])
    arrived(rsq.at[pl.ds(1, len(plane))], q_r.at[0])
    both = jnp.sum(rsq[...], axis=0)
    limit = math.sqrt(D * FF)
    factor = jnp.minimum(1.0, limit / jnp.sqrt(jnp.sum(both, axis=1, keepdims=True) + 1e-06))
    gate_factor, up_factor = factor[0:1], factor[1:2]
    first_scale = 0.003 / (1.0 - 0.9**10)
    second_scale = 1.0 / (1.0 - 0.95**10)

    def moments(g, slot):
        clipped = jnp.concatenate([g[:, :FF] * gate_factor, g[:, FF:] * up_factor], axis=1)
        return 0.9 * pw[1, slot] + 0.1 * clipped, 0.95 * pw[2, slot] + 0.05 * clipped * clipped

    for o in range(NZ):
        k = at_z(NZ - o)
        first, second = moments(gz[o].astype(f32), k)
        low = pw[0, k] * (1.0 - 0.003 * 0.1) - (first * first_scale) / (jnp.sqrt(second * second_scale) + 1e-08)
        low = low.astype(bf16)
        wa[x, c, k, y] = low[:, :FF]
        wb[x, c, k, y] = low[:, FF:]

    def pa(ox, oy, lo=0, n=NZ):
        return wa.at[at_x(NX - ox), c, pl.ds(lo, n), at_y(NY - oy)]

    def pb(ox, oy, lo=0, n=NZ):
        return wb.at[at_x(NX - ox), c, pl.ds(lo, n), at_y(NY - oy)]

    def to_mate_a(ox, oy):
        send(pa(ox, oy), pa(ox, oy), CA, ca_r.at[ox], mate)

    def to_mate_b(ox, oy):
        send(pb(ox, oy), pb(ox, oy), CB, cb_r.at[ox], mate)

    def spread_a(oy):
        for i, o in enumerate((1, 3)):
            send(pa(0, oy), pa(0, oy), GA, na_r.at[i, oy], xp(o))
        to_mate_a(0, oy)

    def spread_b(ox):
        for i, o in enumerate((1, 3)):
            send(pb(ox, 0), pb(ox, 0), GB, nb_r.at[i, ox], yp(o))
        to_mate_b(ox, 0)

    for o in (1, 3, 2):
        send(pa(0, 0), pa(0, 0), GA, ga_r.at[o - 1], yp(o))
        send(pb(0, 0), pb(0, 0), GB, gb_r.at[o - 1], xp(o))
    spread_a(0)
    spread_b(0)

    first, second = moments(grad, z)
    nf_ref[...] = first
    nv_ref[...] = second

    def forward(o):
        arrived(pa(0, o), ga_r.at[o - 1])
        spread_a(o)
        arrived(pb(o, 0), gb_r.at[o - 1])
        spread_b(o)

    def relay(k):
        for i, o in enumerate((1, 3)):
            arrived(pa(o, k), na_r.at[i, k])
            part = pa(o, k, i * half, half)
            send(part, part, GA, ha_r.at[k], xp(o))
            to_mate_a(o, k)
            arrived(pb(k, o), nb_r.at[i, k])
            part = pb(k, o, i * half, half)
            send(part, part, GB, hb_r.at[k], yp(o))
            to_mate_b(k, o)

    def last(k):
        arrived(pa(2, k), ha_r.at[k])
        to_mate_a(2, k)
        arrived(pb(k, 2), hb_r.at[k])
        to_mate_b(k, 2)

    wa_k, wb_k = wa.reshape(NX, 512, FF), wb.reshape(NX, 512, FF)
    def mate_a(ox):
        arrived(wa.at[at_x(NX - ox), other], ca_r.at[ox])

    def mate_b(ox):
        arrived(wb.at[at_x(NX - ox), other], cb_r.at[ox])

    tile_rows = 512

    tile_rows = 512

    def multiply(acc, w_k, *oxs):
        ks = [at_x(NX - ox) for ox in oxs]

        def tile(i, _):
            r = pl.ds(pl.multiple_of(i * tile_rows, tile_rows), tile_rows)
            terms = [jnp.dot(nxt[k, r, :], w_k[k], preferred_element_type=f32) for k in ks]
            acc[r, :] = sum(terms[1:], terms[0]) if 0 in oxs else sum(terms, acc[r, :])
            return 0

        lax.fori_loop(0, TOK // tile_rows, tile, 0)

    def finish():
        k = at_x(NX - 2)

        def tile(i, _):
            r = pl.ds(pl.multiple_of(i * tile_rows, tile_rows), tile_rows)
            gate = gate_acc[r, :] + jnp.dot(nxt[k, r, :], wa_k[k], preferred_element_type=f32)
            up = up_acc[r, :] + jnp.dot(nxt[k, r, :], wb_k[k], preferred_element_type=f32)
            out_ref[r, :] = (gate / (1.0 + jnp.exp(-gate)) * up).astype(bf16)
            return 0

        lax.fori_loop(0, TOK // tile_rows, tile, 0)

    forward(1)
    forward(3)
    relay(0)
    forward(2)
    pltpu.make_async_copy(nxt, nxt, ld.at[5]).wait()
    relay(1)
    mate_a(0)
    multiply(gate_acc, wa_k, 0)
    relay(3)
    relay(2)
    last(0)
    last(1)
    mate_b(0)
    multiply(up_acc, wb_k, 0)
    last(3)
    mate_a(1)
    mate_a(3)
    multiply(gate_acc, wa_k, 1, 3)
    last(2)
    mate_b(1)
    mate_b(3)
    multiply(up_acc, wb_k, 1, 3)
    mate_a(2)
    mate_b(2)
    finish()
    kib = nxt.reshape(NX * TOK, 512)
    piece = NZ * ROWS
    reduced = 2048 + (12 + 12 + 3 + 3) * piece
    rest = (2 * 16 + 96) * (NZ - 1) + (15 + 15 + 16) * piece
    for kind, n in enumerate((reduced, rest, 16 * piece)):
        handle(kib.at[pl.ds(0, n)], done.at[kind]).wait_send()
    handle(rsqz, done.at[QZ]).wait_send()
    handle(rsq.at[pl.ds(1, len(plane))], done.at[Q]).wait_send()


def keep(a_ref, b_ref, c_ref, a_out, b_out, c_out, sem):
    moves = ((c_ref, c_out), (a_ref, a_out), (b_ref, b_out))
    copies = [pltpu.make_async_copy(s, d, sem.at[i]) for i, (s, d) in enumerate(moves)]
    for cp in copies:
        cp.start()
    for cp in copies:
        cp.wait()


def shards(tokens, grad_out, master_weight, first_moment, second_moment, next_tokens):
    any_ = pl.BlockSpec(memory_space=pltpu.HBM)
    V = pltpu.VMEM
    dma = pltpu.SemaphoreType.DMA

    block = (NX, 2, NZ, NY, ROWS, FF)
    piece = (NZ, ROWS, FF)
    scratch = [
        V((2 * NX, TOK, 256), bf16), V((2, TOK, FF), bf16), V((NX, TOK, 512), bf16), V((3, NZ, ROWS, 2 * FF), f32),
        V(block, f32), V(block, bf16), V(block, bf16),
        V((NX - 1, NY, *piece), bf16), V((NX, NY - 1, *piece), bf16), V((2, 2, *piece), bf16), V((NX, *piece), bf16),
        V((NY, 2, *piece), bf16), V((NX, 2, *piece), bf16),
        V((NY - 1, *piece), bf16), V((NX - 1, *piece), bf16), V((NY - 1, *piece), bf16), V((NX - 1, *piece), bf16),
        V((NZ, ROWS, 2 * FF), bf16), V((NZ - 1, ROWS, 2 * FF), bf16),
        V((2, 128), f32), V((NZ - 1, 2, 128), f32), V((NX * NC * NY, 2, 128), f32),
        V((NZ, ROWS, 2 * FF), bf16),
        V((NX, NC, NZ, NY, ROWS, FF), bf16), V((NX, NC, NZ, NY, ROWS, FF), bf16),
        V((TOK, FF), f32), V((TOK, FF), f32),
        dma((2 * NX,)), dma((6,)), dma((5,)),
        dma((NX, 2)), dma((2,)), dma((NX,)), dma((NY,)), dma((NX,)), dma((1,)), dma((1,)), dma((1,)),
        dma((NZ - 1,)), dma((1,)), dma((1,)), dma((1,)),
        dma((NY - 1,)), dma((NX - 1,)), dma((2, NY)), dma((2, NX)), dma((NY,)), dma((NX,)), dma((NX,)), dma((NX,)),
    ]
    shapes = (
        jax.ShapeDtypeStruct((ROWS, 2 * FF), f32),
        jax.ShapeDtypeStruct((ROWS, 2 * FF), f32),
        jax.ShapeDtypeStruct((TOK, FF), bf16),
    )
    inputs = (tokens, grad_out, master_weight, first_moment, second_moment, next_tokens)
    results = pl.pallas_call(
        body,
        out_shape=shapes,
        in_specs=[any_] * 6,
        out_specs=(pl.BlockSpec(memory_space=pltpu.VMEM),) * 3,
        scratch_shapes=scratch,
        compiler_params=pltpu.CompilerParams(
            collective_id=0, has_side_effects=True, vmem_limit_bytes=103 * 512 * 1024
        ),
    )(*(pltpu.with_memory_space_constraint(a, pltpu.HBM) for a in inputs))
    return pl.pallas_call(
        keep,
        out_shape=shapes,
        in_specs=[any_] * 3,
        out_specs=(any_,) * 3,
        scratch_shapes=[dma((3,))],
        compiler_params=pltpu.CompilerParams(vmem_limit_bytes=2 * 1024 * 1024),
    )(*results)


def solution(mesh):
    split = Mesh(mesh.devices.reshape(NX, NC, NZ, NY), AXES)
    rows = P(AXES, None)
    return jax.shard_map(
        shards, mesh=split, in_specs=(rows,) * 6, out_specs=(rows,) * 3, check_vma=False
    )
```

```python
import math

import jax
import jax.numpy as jnp
from jax import lax
from jax.experimental import pallas as pl
from jax.experimental.pallas import tpu as pltpu
from jax.sharding import Mesh
from jax.sharding import PartitionSpec as P

NX, NC, NZ, NY = 4, 2, 8, 4
ROWS = 8
D = 2048
FF = 512
TOK = 1024
AXES = ("x", "c", "z", "y")
MESH = pl.DeviceIdType.MESH
FAR_Z = (4, 3, 5, 2, 6, 1, 7)
f32 = jnp.float32
bf16 = jnp.bfloat16


def body(
    tok_hbm, cot_hbm, w_hbm, m_hbm, v_hbm, nxt_hbm,
    nf_ref, nv_ref, out_ref,
    tok, cot, nxt, pw, own, give, take,
    sa, sb, fa, fb, ra1, rb1, ta, tb, ra2, rb2, tz, rz, sqz, rsqz, rsq, gz, wa, wb, gate_acc, up_acc,
    ld_t, ld, done, core_r, fa_r, fb_r, a1_r, b1_r, a2_r, b2_r, z_r, pw_r, qz_r, q_r, g_r,
    ga_r, gb_r, na_r, nb_r, ha_r, hb_r, ca_r, cb_r,
):
    x, c, z, y = (lax.axis_index(a) for a in AXES)
    other = 1 - c

    def at_x(o):
        return lax.rem(x + o, NX)

    def at_y(o):
        return lax.rem(y + o, NY)

    def at_z(o):
        return lax.rem(z + o, NZ)

    def xp(o):
        return {"x": at_x(o)}

    def yp(o):
        return {"y": at_y(o)}

    def zp(o):
        return {"z": at_z(o)}

    mate = {"c": other}
    plane = [
        (ox, oc, oy) for ox in (2, 1, 3, 0) for oy in (2, 1, 3, 0) for oc in (1, 0) if ox or oc or oy
    ]

    def in_plane(ox, oc, oy):
        return {"x": at_x(ox), "c": other if oc else c, "y": at_y(oy)}

    CORE = A1 = B1 = A2 = B2 = 0
    Z = PW = G = GA = GB = CA = 1
    CB, QZ, Q = 2, 3, 4

    def send(src, dst, kind, rs, to):
        pltpu.make_async_remote_copy(
            src_ref=src, dst_ref=dst, send_sem=done.at[kind], recv_sem=rs, device_id=to, device_id_type=MESH
        ).start()

    def handle(ref, sem):
        return pltpu.make_async_remote_copy(
            src_ref=ref, dst_ref=ref, send_sem=sem, recv_sem=sem, device_id=mate, device_id_type=MESH
        )

    def arrived(dst, rs):
        handle(dst, rs).wait_recv()

    barrier = pltpu.get_barrier_semaphore()
    for o in plane:
        pl.semaphore_signal(barrier, inc=1, device_id=in_plane(*o), device_id_type=MESH)
    for o in FAR_Z:
        pl.semaphore_signal(barrier, inc=1, device_id=zp(o), device_id_type=MESH)

    offs = (2, 1, 3, 0)
    blocks = [at_x(o) for o in offs]
    load_cot = [
        pltpu.make_async_copy(cot_hbm.at[:, pl.ds(i * FF, FF)], cot.at[i], ld.at[3 + i]) for i in range(2)
    ]
    load_tok = []
    for j in range(NX):
        for i, cc in enumerate((other, c)):
            start = pl.multiple_of(blocks[j] * 512 + cc * 256, 256)
            load_tok.append(
                pltpu.make_async_copy(tok_hbm.at[:, pl.ds(start, 256)], tok.at[2 * j + i], ld_t.at[2 * j + i])
            )
    load_pw = [
        pltpu.make_async_copy(h, pw.at[i, z], ld.at[i]) for i, h in enumerate((w_hbm, m_hbm, v_hbm))
    ]
    load_nxt = [
        pltpu.make_async_copy(nxt_hbm.at[:, pl.ds(k * 512, 512)], nxt.at[k], ld.at[5]) for k in range(NX)
    ]
    for cp in [load_cot[0], load_tok[0], load_cot[1], load_tok[1]]:
        cp.start()

    def rows_of(i):
        return jnp.transpose(tok[i])

    def block_grad(lhs, h):
        return jnp.dot(lhs, cot[h], preferred_element_type=f32).reshape(NZ, NY, ROWS, FF)

    def pass_on(src, o, to):
        slot = at_z(NZ - src)
        send(pw.at[:, slot], pw.at[:, slot], PW, pw_r.at[o - 1], zp(to))

    half = NZ // 2
    lower, upper = pl.ds(0, half), pl.ds(half, half)
    whole = pl.ds(0, NZ)
    via_next, via_prev = (2, 0), (1, 3)

    def gate_sum(j, k, zs=whole):
        yk = at_y(k)
        return own[j, 0, zs, yk] + take[j, 0, zs, yk].astype(f32)

    def up_sum(j, k, zs=whole):
        yk = at_y(k)
        return own[j, 1, zs, yk] + take[j, 1, zs, yk].astype(f32)

    def near_a(j, k, value):
        sa[j, k] = value.astype(bf16)
        send(sa.at[j, k], ra1.at[k, j - 1], A1, a1_r.at[k], xp(1 if j == 1 else 3))

    def near_b(j, i, zs, value):
        sb[j, 1 + i, zs] = value.astype(bf16)
        send(sb.at[j, 1 + i, zs], rb1.at[j, i, zs], B1, b1_r.at[j], yp((1, 3)[i]))

    def combine_gate(j):
        arrived(take.at[j, 0], core_r.at[j, 0])
        if j == 0:
            for k in (2, 1, 0, 3):
                sa[0, k] = gate_sum(0, k).astype(bf16)
                i, n = (0, via_next.index(k)) if k in via_next else (1, via_prev.index(k))
                send(sa.at[0, k], fa.at[i, n], A1, fa_r.at[i], xp(1 if i == 0 else 3))
        if j == 1:
            for k in via_prev:
                near_a(1, k, gate_sum(1, k))
        if j == 2:
            near_a(2, 2, gate_sum(2, 2))

    def combine_up(j):
        arrived(take.at[j, 1], core_r.at[j, 1])
        sb[j, 0] = up_sum(j, 2).astype(bf16)
        for zs, o in ((lower, 1), (upper, 3)):
            send(sb.at[j, 0, zs], fb.at[j, zs], B1, fb_r.at[j], yp(o))
        near_b(j, 0, upper, up_sum(j, 1, upper))
        near_b(j, 1, lower, up_sum(j, 3, lower))

    def add_a(i):
        arrived(fa.at[i], fa_r.at[i])
        for n, k in enumerate((via_next, via_prev)[i]):
            near_a(1 + i, k, gate_sum(1 + i, k) + fa[i, n].astype(f32))

    def add_b(j):
        arrived(fb.at[j], fb_r.at[j])
        near_b(j, 0, lower, up_sum(j, 1, lower) + fb[j, lower].astype(f32))
        near_b(j, 1, upper, up_sum(j, 3, upper) + fb[j, upper].astype(f32))

    def second_a(k):
        total = gate_sum(NX - 1, k)
        arrived(ra1.at[k], a1_r.at[k])
        total += ra1[k, 0].astype(f32) + ra1[k, 1].astype(f32)
        if k:
            ta[k - 1] = total.astype(bf16)
            send(ta.at[k - 1], ra2.at[k - 1], A2, a2_r.at[0], yp(k))
        return total

    def second_b(j):
        total = up_sum(j, 0)
        arrived(rb1.at[j], b1_r.at[j])
        total += rb1[j, 0].astype(f32) + rb1[j, 1].astype(f32)
        o = offs[j]
        if o:
            tb[o - 1] = total.astype(bf16)
            send(tb.at[o - 1], rb2.at[o - 1], B2, b2_r.at[0], xp(o))
        return total

    def give_send(j, h):
        send(give.at[j, h], take.at[j, h], CORE, core_r.at[j, h], mate)

    for j in range(NX):
        if j:
            load_tok[2 * j].wait()
        else:
            load_cot[0].wait()
            load_tok[0].wait()
            for cp in load_tok[2:] + load_pw:
                cp.start()
        lhs = rows_of(2 * j)
        give[j, 0] = block_grad(lhs, 0).astype(bf16)
        if j == 0:
            pl.semaphore_wait(barrier, len(plane) + len(FAR_Z))
        give_send(j, 0)
        if j == 0:
            load_cot[1].wait()
        give[j, 1] = block_grad(lhs, 1).astype(bf16)
        give_send(j, 1)
        if j:
            combine_gate(j - 1)
            combine_up(j - 1)
        if j == NX - 1:
            add_b(0)
        load_tok[2 * j + 1].wait()
        lhs = rows_of(2 * j + 1)
        own[j, 0] = block_grad(lhs, 0)
        own[j, 1] = block_grad(lhs, 1)
        if j == 0:
            for cp in load_pw:
                cp.wait()
            pass_on(0, 1, 1)
            pass_on(0, 7, 7)
            pass_on(0, 4, 4)
    combine_gate(NX - 1)
    add_b(1)
    add_a(0)
    add_a(1)
    near_a(2, 0, gate_sum(2, 0))
    add_b(2)
    combine_up(NX - 1)
    for cp in load_nxt:
        cp.start()
    arrived(pw.at[:, at_z(7)], pw_r.at[0])
    pass_on(1, 2, 1)
    arrived(pw.at[:, at_z(1)], pw_r.at[6])
    pass_on(7, 6, 7)
    second_b(0)
    second_a(2)
    add_b(3)
    second_b(1)
    second_a(1)
    second_b(2)
    second_a(3)
    total = second_a(0)
    arrived(pw.at[:, at_z(6)], pw_r.at[1])
    pass_on(2, 3, 1)
    arrived(pw.at[:, at_z(2)], pw_r.at[5])
    pass_on(6, 5, 7)
    arrived(ra2, a2_r.at[0])
    for k in range(NY - 1):
        total += ra2[k].astype(f32)
    tz[:, :, :FF] = total.astype(bf16)
    total = second_b(NX - 1)
    arrived(rb2, b2_r.at[0])
    for k in range(NX - 1):
        total += rb2[k].astype(f32)
    tz[:, :, FF:] = total.astype(bf16)

    for o in FAR_Z:
        send(tz.at[at_z(o)], rz.at[o - 1], Z, z_r.at[0], zp(o))
    grad = tz[z].astype(f32)
    arrived(rz, z_r.at[0])
    for o in range(NZ - 1):
        grad += rz[o].astype(f32)

    def fold(t):
        t = t * t
        t = jnp.sum(t, axis=0, keepdims=True)
        return t[:, 0:128] + t[:, 128:256] + t[:, 256:384] + t[:, 384:512]

    sqz[...] = jnp.concatenate([fold(grad[:, :FF]), fold(grad[:, FF:])], axis=0)
    for o in FAR_Z:
        send(sqz, rsqz.at[o - 1], QZ, qz_r.at[0], zp(o))
    gz[0] = grad.astype(bf16)
    both = sqz[...]
    arrived(rsqz, qz_r.at[0])
    for o in range(NZ - 1):
        both += rsqz[o]
    rsq[0] = both
    for i, o in enumerate(plane):
        send(rsq.at[0], rsq.at[1 + i], Q, q_r.at[0], in_plane(*o))
    for o in FAR_Z:
        send(gz.at[0], gz.at[o], G, g_r.at[0], zp(o))
    arrived(gz.at[pl.ds(1, NZ - 1)], g_r.at[0])
    for o in (3, 5, 4):
        arrived(pw.at[:, at_z(NZ - o)], pw_r.at[o - 1])
    arrived(rsq.at[pl.ds(1, len(plane))], q_r.at[0])
    both = jnp.sum(rsq[...], axis=0)
    limit = math.sqrt(D * FF)
    factor = jnp.minimum(1.0, limit / jnp.sqrt(jnp.sum(both, axis=1, keepdims=True) + 1e-06))
    gate_factor, up_factor = factor[0:1], factor[1:2]
    first_scale = 0.003 / (1.0 - 0.9**10)
    second_scale = 1.0 / (1.0 - 0.95**10)

    def moments(g, slot):
        clipped = jnp.concatenate([g[:, :FF] * gate_factor, g[:, FF:] * up_factor], axis=1)
        return 0.9 * pw[1, slot] + 0.1 * clipped, 0.95 * pw[2, slot] + 0.05 * clipped * clipped

    def low_rows(dst, h, scale):
        cols = pl.ds(h * FF, FF)
        for o in range(NZ):
            k = at_z(NZ - o)
            clipped = gz[o, :, cols].astype(f32) * scale
            first = 0.9 * pw[1, k, :, cols] + 0.1 * clipped
            second = 0.95 * pw[2, k, :, cols] + 0.05 * clipped * clipped
            low = pw[0, k, :, cols] * (1.0 - 0.003 * 0.1) - (first * first_scale) / (
                jnp.sqrt(second * second_scale) + 1e-08
            )
            dst[x, c, k, y] = low.astype(bf16)

    def pa(ox, oy, lo=0, n=NZ):
        return wa.at[at_x(NX - ox), c, pl.ds(lo, n), at_y(NY - oy)]

    def pb(ox, oy, lo=0, n=NZ):
        return wb.at[at_x(NX - ox), c, pl.ds(lo, n), at_y(NY - oy)]

    def to_mate_a(ox, oy):
        send(pa(ox, oy), pa(ox, oy), CA, ca_r.at[ox], mate)

    def to_mate_b(ox, oy):
        send(pb(ox, oy), pb(ox, oy), CB, cb_r.at[ox], mate)

    def spread_a(oy):
        for i, o in enumerate((1, 3)):
            send(pa(0, oy), pa(0, oy), GA, na_r.at[i, oy], xp(o))
        to_mate_a(0, oy)

    def spread_b(ox):
        for i, o in enumerate((1, 3)):
            send(pb(ox, 0), pb(ox, 0), GB, nb_r.at[i, ox], yp(o))
        to_mate_b(ox, 0)

    low_rows(wa, 0, gate_factor)
    for o in (1, 3, 2):
        send(pa(0, 0), pa(0, 0), GA, ga_r.at[o - 1], yp(o))
    spread_a(0)
    low_rows(wb, 1, up_factor)
    for o in (1, 3, 2):
        send(pb(0, 0), pb(0, 0), GB, gb_r.at[o - 1], xp(o))
    spread_b(0)

    first, second = moments(grad, z)
    nf_ref[...] = first
    nv_ref[...] = second

    def forward(o):
        arrived(pa(0, o), ga_r.at[o - 1])
        spread_a(o)
        arrived(pb(o, 0), gb_r.at[o - 1])
        spread_b(o)

    def relay(k):
        for i, o in enumerate((1, 3)):
            arrived(pa(o, k), na_r.at[i, k])
            part = pa(o, k, i * half, half)
            send(part, part, GA, ha_r.at[k], xp(o))
            to_mate_a(o, k)
            arrived(pb(k, o), nb_r.at[i, k])
            part = pb(k, o, i * half, half)
            send(part, part, GB, hb_r.at[k], yp(o))
            to_mate_b(k, o)

    def last(k):
        arrived(pa(2, k), ha_r.at[k])
        to_mate_a(2, k)
        arrived(pb(k, 2), hb_r.at[k])
        to_mate_b(k, 2)

    wa_k, wb_k = wa.reshape(NX, 512, FF), wb.reshape(NX, 512, FF)
    def mate_a(ox):
        arrived(wa.at[at_x(NX - ox), other], ca_r.at[ox])

    def mate_b(ox):
        arrived(wb.at[at_x(NX - ox), other], cb_r.at[ox])

    tile_rows = 512

    tile_rows = 512

    def multiply(acc, w_k, *oxs):
        ks = [at_x(NX - ox) for ox in oxs]

        def tile(i, _):
            r = pl.ds(pl.multiple_of(i * tile_rows, tile_rows), tile_rows)
            terms = [jnp.dot(nxt[k, r, :], w_k[k], preferred_element_type=f32) for k in ks]
            acc[r, :] = sum(terms[1:], terms[0]) if 0 in oxs else sum(terms, acc[r, :])
            return 0

        lax.fori_loop(0, TOK // tile_rows, tile, 0)

    def finish():
        k = at_x(NX - 2)

        def tile(i, _):
            r = pl.ds(pl.multiple_of(i * tile_rows, tile_rows), tile_rows)
            gate = gate_acc[r, :] + jnp.dot(nxt[k, r, :], wa_k[k], preferred_element_type=f32)
            up = up_acc[r, :] + jnp.dot(nxt[k, r, :], wb_k[k], preferred_element_type=f32)
            out_ref[r, :] = (gate / (1.0 + jnp.exp(-gate)) * up).astype(bf16)
            return 0

        lax.fori_loop(0, TOK // tile_rows, tile, 0)

    forward(1)
    forward(3)
    relay(0)
    forward(2)
    pltpu.make_async_copy(nxt, nxt, ld.at[5]).wait()
    relay(1)
    mate_a(0)
    multiply(gate_acc, wa_k, 0)
    relay(3)
    relay(2)
    last(0)
    last(1)
    mate_b(0)
    multiply(up_acc, wb_k, 0)
    last(3)
    mate_a(1)
    mate_a(3)
    multiply(gate_acc, wa_k, 1, 3)
    last(2)
    mate_b(1)
    mate_b(3)
    multiply(up_acc, wb_k, 1, 3)
    mate_a(2)
    mate_b(2)
    finish()
    kib = nxt.reshape(NX * TOK, 512)
    piece = NZ * ROWS
    reduced = 2048 + (12 + 12 + 3 + 3) * piece
    rest = (2 * 16 + 96) * (NZ - 1) + (15 + 15 + 16) * piece
    for kind, n in enumerate((reduced, rest, 16 * piece)):
        handle(kib.at[pl.ds(0, n)], done.at[kind]).wait_send()
    handle(rsqz, done.at[QZ]).wait_send()
    handle(rsq.at[pl.ds(1, len(plane))], done.at[Q]).wait_send()


def keep(a_ref, b_ref, c_ref, a_out, b_out, c_out, sem):
    moves = ((c_ref, c_out), (a_ref, a_out), (b_ref, b_out))
    copies = [pltpu.make_async_copy(s, d, sem.at[i]) for i, (s, d) in enumerate(moves)]
    for cp in copies:
        cp.start()
    for cp in copies:
        cp.wait()


def shards(tokens, grad_out, master_weight, first_moment, second_moment, next_tokens):
    any_ = pl.BlockSpec(memory_space=pltpu.HBM)
    V = pltpu.VMEM
    dma = pltpu.SemaphoreType.DMA

    block = (NX, 2, NZ, NY, ROWS, FF)
    piece = (NZ, ROWS, FF)
    scratch = [
        V((2 * NX, TOK, 256), bf16), V((2, TOK, FF), bf16), V((NX, TOK, 512), bf16), V((3, NZ, ROWS, 2 * FF), f32),
        V(block, f32), V(block, bf16), V(block, bf16),
        V((NX - 1, NY, *piece), bf16), V((NX, NY - 1, *piece), bf16), V((2, 2, *piece), bf16), V((NX, *piece), bf16),
        V((NY, 2, *piece), bf16), V((NX, 2, *piece), bf16),
        V((NY - 1, *piece), bf16), V((NX - 1, *piece), bf16), V((NY - 1, *piece), bf16), V((NX - 1, *piece), bf16),
        V((NZ, ROWS, 2 * FF), bf16), V((NZ - 1, ROWS, 2 * FF), bf16),
        V((2, 128), f32), V((NZ - 1, 2, 128), f32), V((NX * NC * NY, 2, 128), f32),
        V((NZ, ROWS, 2 * FF), bf16),
        V((NX, NC, NZ, NY, ROWS, FF), bf16), V((NX, NC, NZ, NY, ROWS, FF), bf16),
        V((TOK, FF), f32), V((TOK, FF), f32),
        dma((2 * NX,)), dma((6,)), dma((5,)),
        dma((NX, 2)), dma((2,)), dma((NX,)), dma((NY,)), dma((NX,)), dma((1,)), dma((1,)), dma((1,)),
        dma((NZ - 1,)), dma((1,)), dma((1,)), dma((1,)),
        dma((NY - 1,)), dma((NX - 1,)), dma((2, NY)), dma((2, NX)), dma((NY,)), dma((NX,)), dma((NX,)), dma((NX,)),
    ]
    shapes = (
        jax.ShapeDtypeStruct((ROWS, 2 * FF), f32),
        jax.ShapeDtypeStruct((ROWS, 2 * FF), f32),
        jax.ShapeDtypeStruct((TOK, FF), bf16),
    )
    inputs = (tokens, grad_out, master_weight, first_moment, second_moment, next_tokens)
    results = pl.pallas_call(
        body,
        out_shape=shapes,
        in_specs=[any_] * 6,
        out_specs=(pl.BlockSpec(memory_space=pltpu.VMEM),) * 3,
        scratch_shapes=scratch,
        compiler_params=pltpu.CompilerParams(
            collective_id=0, has_side_effects=True, vmem_limit_bytes=103 * 512 * 1024
        ),
    )(*(pltpu.with_memory_space_constraint(a, pltpu.HBM) for a in inputs))
    return pl.pallas_call(
        keep,
        out_shape=shapes,
        in_specs=[any_] * 3,
        out_specs=(any_,) * 3,
        scratch_shapes=[dma((3,))],
        compiler_params=pltpu.CompilerParams(vmem_limit_bytes=2 * 1024 * 1024),
    )(*results)


def solution(mesh):
    split = Mesh(mesh.devices.reshape(NX, NC, NZ, NY), AXES)
    rows = P(AXES, None)
    return jax.shard_map(
        shards, mesh=split, in_specs=(rows,) * 6, out_specs=(rows,) * 3, check_vma=False
    )
```
